256 devices in a mesh: frames: 16 (over y_lo, x, core), rows: 16 (over y_hi, z).
Axes of the slice: x: 4, y: 4 (y_hi: 2, y_lo: 2; y = y_hi * 2 + y_lo), z: 8, core: 2. Of those that a mesh axis runs over, the one named last changes fastest.
Arguments:
- video: bfloat16 [16, 64, 320, 192], P('frames', 'rows'), may hold values from -6 to 6
- spatial_weights: bfloat16 [4, 3, 3, 192, 192], replicated, may hold values from -0.15625 to 0.15625
- norm_gains: float32 [4, 192], replicated, may hold values from 0.5 to 1.5
- temporal_weights: bfloat16 [2, 3, 192, 192], replicated, may hold values from -0.25 to 0.25
Outputs:
- decoded: bfloat16 [16, 64, 320, 192], P('frames', 'rows')
The draws below stay inside these ranges and needn't reach their ends.
All inputs are finite; a program needn't handle non-finite values.
Results may differ from the reference program's by a relative error of at most 0.013.
Values may be sent and summed in bfloat16 or wider, within the bound.
No kernel may reach another device: no remote copies, remote signals or barrier semaphores. Data moves between devices by JAX's collectives and lax.ppermute only.
A program may use at most 64 MiB of HBM per device.

```python
import jax
import jax.numpy as jnp
from jax import lax

C = 192
W = 320
BLOCKS = 2
H = 64
FRAMES = 16


def level_of(stream_key, extent, pieces, low, high):
    def one(axis_at, shards_of):
        draws = jax.random.uniform(jax.random.fold_in(jax.random.fold_in(stream_key, 6), axis_at), (shards_of,), jnp.float32, low / len(pieces), high / len(pieces))
        return jnp.repeat(jnp.exp(draws), extent[axis_at] // shards_of).reshape((-1,) + (1,) * (len(extent) - axis_at - 1))

    factor_of = one(*pieces[0])
    for cut in pieces[1:]:
        factor_of = factor_of * one(*cut)
    return factor_of


def scatter_about(stream_key, shape, deviation, limit, cuts=(), kind=jnp.bfloat16):
    array = jax.random.normal(stream_key, shape, jnp.float32) * deviation
    if len(cuts) > 0:
        array = level_of(stream_key, shape, cuts, -0.22, 0.18) * array
    return jnp.clip(array, min=-limit, max=limit).astype(kind)


def setup_inputs(seed: int = 0) -> dict:
    keys = jax.random.split(jax.random.key(seed), 5)
    video = scatter_about(keys[0], (FRAMES, H, W, C), 1.0, 6.0, ((0, 16), (1, 16)))
    spatial_weights = scatter_about(keys[1], (2 * BLOCKS, 3, 3, C, C), (9 * C) ** -0.5, 0.15625)
    norm_gains = jnp.clip(jax.random.uniform(keys[2], (2 * BLOCKS, C), jnp.float32, 0.5, 1.5), 0.5, 1.5)
    temporal_weights = scatter_about(keys[3], (BLOCKS, 3, C, C), (3 * C) ** -0.5, 0.25)
    return {"video": video, "spatial_weights": spatial_weights, "norm_gains": norm_gains, "temporal_weights": temporal_weights}


epsilon = 1e-06

def normed(values, gain):
    values = values.astype(jnp.float32)
    mean_sq = lax.optimization_barrier(jnp.mean(values * values, axis=-1, keepdims=True))
    scaled = values * lax.rsqrt(mean_sq + epsilon) * gain.astype(jnp.float32)
    return jax.nn.silu(scaled).astype(jnp.bfloat16)

def conv_frame(active, kernel):
    height, width, channels = active.shape
    padded = jnp.pad(active.astype(jnp.float32), ((1, 1), (1, 1), (0, 0)))
    total = jnp.zeros((height * width, kernel.shape[-1]), jnp.float32)
    for row_step in range(3):
        for col_step in range(3):
            window = padded[row_step:row_step + height, col_step:col_step + width].reshape(-1, channels)
            total = total + jnp.dot(window, kernel[row_step, col_step].astype(jnp.float32), preferred_element_type=jnp.float32)
    return total.reshape(height, width, kernel.shape[-1])

def reference(video, spatial_weights, norm_gains, temporal_weights):
    current = video
    for block in range(BLOCKS):

        def spatial(frame):
            first = conv_frame(normed(frame, norm_gains[2 * block]), spatial_weights[2 * block]).astype(jnp.bfloat16)
            second = conv_frame(normed(first, norm_gains[2 * block + 1]), spatial_weights[2 * block + 1])
            return (frame.astype(jnp.float32) + second).astype(jnp.bfloat16)
        inner = lax.map(spatial, current)
        padded = jnp.concatenate([jnp.zeros((2,) + inner.shape[1:], jnp.bfloat16), inner], axis=0)

        def temporal(index):
            taps = lax.dynamic_slice_in_dim(padded, index, 3, 0)
            height, width, channels = taps.shape[1:]
            total = taps[2].astype(jnp.float32).reshape(-1, channels)
            for offset in range(3):
                total = total + jnp.dot(taps[2 - offset].astype(jnp.float32).reshape(-1, channels), temporal_weights[block, offset].astype(jnp.float32), preferred_element_type=jnp.float32)
            return total.reshape(height, width, channels).astype(jnp.bfloat16)
        current = lax.map(temporal, jnp.arange(inner.shape[0], dtype=jnp.int32))
    return current
```

```python
import functools

import jax
import jax.numpy as jnp
from jax import lax
from jax.experimental import pallas as pl
from jax.experimental.pallas import tpu as pltpu
from jax.sharding import PartitionSpec as P

C = 192
W = 320
PAIR = 2 * W
LANES = 128
EPS = 1e-06
F32 = jnp.float32
BF16 = jnp.bfloat16
VMEM = pl.BlockSpec(memory_space=pltpu.VMEM)
SMEM = pl.BlockSpec(memory_space=pltpu.SMEM)
LIMIT = 28 << 20


def call(kernel, outs, n_in, name, scratch=(), scalars=True, flops=0, moved=0):
    specs = ([SMEM] if scalars else []) + [VMEM] * n_in
    many = isinstance(outs, (list, tuple))
    return pl.pallas_call(
        kernel,
        out_shape=outs,
        in_specs=specs,
        out_specs=[VMEM] * len(outs) if many else VMEM,
        scratch_shapes=list(scratch),
        compiler_params=pltpu.CompilerParams(vmem_limit_bytes=LIMIT),
        cost_estimate=pl.CostEstimate(flops=flops, bytes_accessed=moved, transcendentals=0),
        name=name,
    )


def pair_shape():
    return jax.ShapeDtypeStruct((C, PAIR), BF16)


def weights_kernel(sw, g, wt, gt):
    for tap in range(9):
        wt[:, tap * C : (tap + 1) * C] = sw[tap // 3, tap % 3].T
    gt[...] = jnp.broadcast_to(g[...] * 0.5, (LANES, C)).T


def prepare(weight, gain):
    return call(
        weights_kernel,
        [jax.ShapeDtypeStruct((C, 9 * C), BF16), jax.ShapeDtypeStruct((C, LANES), F32)],
        2,
        "weights",
        scalars=False,
        moved=1500000,
    )(weight, gain.reshape(1, C))


def taps_kernel(tw, wt):
    for tap in range(3):
        wt[:, tap * C : (tap + 1) * C] = tw[tap].T


def prepare_taps(weight):
    return call(
        taps_kernel, jax.ShapeDtypeStruct((C, 3 * C), BF16), 1, "taps", scalars=False, moved=500000
    )(weight)


def pack_kernel(sc, v, own, sib):
    core = sc[0]
    for dst, pair in ((own, core), (sib, 1 - core)):
        dst[:, :W] = v[2 * pair]
        dst[:, W:] = v[2 * pair + 1]


def unpack_kernel(sc, keep, got, out):
    core = sc[0]
    for src, pair in ((keep, core), (got, 1 - core)):
        out[2 * pair] = src[:, :W]
        out[2 * pair + 1] = src[:, W:]


def activate(x, gain, valid):
    x = x.astype(F32)
    scale = lax.rsqrt(jnp.sum(x * x, axis=0, keepdims=True) * (1.0 / C) + EPS)
    if valid is not None:
        scale = scale * valid
    h = x * scale * gain
    return (h + h * jnp.tanh(h)).astype(BF16)


def column_taps(a):
    col = lax.broadcasted_iota(jnp.int32, (1, PAIR), 1)
    zero = jnp.zeros_like(a)
    left = jnp.where((col == 0) | (col == W), zero, pltpu.roll(a, 1, 1))
    right = jnp.where((col == W - 1) | (col == PAIR - 1), zero, pltpu.roll(a, PAIR - 1, 1))
    return left, a, right


def fill(stack, act, blocks):
    col = lax.broadcasted_iota(jnp.int32, (1, PAIR), 1)
    before = None
    for p in range(blocks):
        taps = column_taps(act[p])
        turned = [pltpu.roll(t, W, 1) for t in taps]
        for dj in range(3):
            if p < blocks - 1:
                stack[dj * C : (dj + 1) * C, p * PAIR : (p + 1) * PAIR] = taps[dj]
            if p > 0:
                q = slice((p - 1) * PAIR, p * PAIR)
                stack[(6 + dj) * C : (7 + dj) * C, q] = taps[dj]
                stack[(3 + dj) * C : (4 + dj) * C, q] = jnp.where(col < W, before[dj], turned[dj])
        before = turned


def spatial_body(sc, load, w1, g1, w2, g2, out, act1, s1, first, act2, s2):
    core, top, bottom = sc[0], sc[1], sc[2]
    for which, block in ((0, 2 * core), (1, 1), (2, 2 - 2 * core)):
        for t in range(PAIR // LANES):
            lanes = slice(t * LANES, (t + 1) * LANES)
            act1[block, :, lanes] = activate(load(which, lanes), g1[...], None)
    fill(s1, act1, 3)
    first[...] = jnp.dot(w1[...], s1[...], preferred_element_type=F32).astype(BF16)
    lane = lax.broadcasted_iota(jnp.int32, (1, LANES), 1)
    for p in range(2):
        for t in range(PAIR // LANES):
            at = p * PAIR + t * LANES
            pixel = lane + at
            outside = ((pixel < W) & (top > 0)) | ((pixel >= 3 * W) & (bottom > 0))
            valid = jnp.where(outside, 0.0, 1.0).astype(F32)
            act2[p, :, t * LANES : (t + 1) * LANES] = activate(
                first[:, at : at + LANES], g2[...], valid
            )
    fill(s2, act2, 2)
    second = jnp.dot(w2[...], s2[...], preferred_element_type=F32)
    out[...] = (load(1, slice(0, PAIR)).astype(F32) + second).astype(BF16)


def spatial_kernel(sc, z, own, sib, w1, g1, w2, g2, out, *scratch):
    refs = (z, own, sib)
    spatial_body(sc, lambda k, lanes: refs[k][:, lanes], w1, g1, w2, g2, out, *scratch)


def spatial_pick_kernel(pick, sc, z0, own0, sib0, z1, own1, sib1, w1, g1, w2, g2, out, *scratch):
    ones, others = (z0, own0, sib0), (z1, own1, sib1)
    mine = sc[0] == pick

    def load(k, lanes):
        return jnp.where(mine, ones[k][:, lanes], others[k][:, lanes])

    spatial_body(sc, load, w1, g1, w2, g2, out, *scratch)


def spatial(kernel, n_in, name):
    return call(
        kernel,
        pair_shape(),
        n_in,
        name,
        scratch=[
            pltpu.VMEM((3, C, PAIR), BF16),
            pltpu.VMEM((9 * C, 2 * PAIR), BF16),
            pltpu.VMEM((C, 2 * PAIR), BF16),
            pltpu.VMEM((2, C, PAIR), BF16),
            pltpu.VMEM((9 * C, PAIR), BF16),
        ],
        flops=2 * C * C * 9 * 3 * PAIR,
        moved=4000000,
    )


def mixed(wt, x0, x1, x2):
    total = x0[...].astype(F32)
    for tap, x in enumerate((x0, x1, x2)):
        total = total + jnp.dot(
            wt[:, tap * C : (tap + 1) * C], x[...], preferred_element_type=F32
        )
    return total.astype(BF16)


def temporal_kernel(wt, x0, x1, x2, out):
    out[...] = mixed(wt, x0, x1, x2)


def temporal(wt, x0, x1, x2):
    return call(
        temporal_kernel,
        pair_shape(),
        4,
        "temporal",
        scalars=False,
        flops=2 * C * C * 3 * PAIR,
        moved=1300000,
    )(wt, x0, x1, x2)


def temporal_last_kernel(sc, wt, x0, x1, x2, late, keep, send):
    early = mixed(wt, x0, x1, x2)
    is0 = sc[0] == 0
    other = late[...]
    keep[...] = jnp.where(is0, early, other)
    send[...] = jnp.where(is0, other, early)


def on_device(video, spatial_weights, norm_gains, temporal_weights):
    frames, rows = lax.axis_size("frames"), lax.axis_size("rows")
    core = lax.axis_index("frames") % 2
    row = lax.axis_index("rows")
    top = (core == 0) & (row == 0)
    bottom = (core == 1) & (row == rows - 1)
    sc = jnp.stack([core, top, bottom]).astype(jnp.int32)

    swaps = [(i, i ^ 1) for i in range(frames)]
    across = []
    for f in range(frames):
        for r in range(rows):
            to = r + 1 if f % 2 else r - 1
            if 0 <= to < rows:
                across.append((f * rows + r, (f ^ 1) * rows + to))
    later = [(i, i + 2) for i in range(frames - 2)]

    def swap(x):
        return lax.ppermute(x, "frames", swaps)

    def halo(x):
        return lax.ppermute(x, ("frames", "rows"), across)

    def onward(x):
        return lax.ppermute(x, "frames", later)

    view = jnp.transpose(video[0], (0, 2, 1))
    own_m, sib_m = call(pack_kernel, [pair_shape()] * 2, 1, "pack", moved=1000000)(sc, view)
    own_o = swap(sib_m)
    sib_o = swap(own_m)
    z_o = halo(own_m)
    z_m = halo(own_o)
    ws = [prepare(spatial_weights[k], norm_gains[k]) for k in range(4)]
    ts = [prepare_taps(temporal_weights[k]) for k in range(2)]

    weights = (*ws[0], *ws[1])
    arrays = (z_m, own_m, sib_m, z_o, own_o, sib_o)
    inner_b = spatial(functools.partial(spatial_pick_kernel, 1), 10, "spatial_b")(sc, *arrays, *weights)
    before_b = onward(inner_b)
    inner_a = spatial(functools.partial(spatial_pick_kernel, 0), 10, "spatial_a")(sc, *arrays, *weights)
    before_a = onward(inner_a)
    own_b = temporal(ts[0], inner_b, inner_a, before_b)
    sib_b, z_b = swap(own_b), halo(own_b)
    own_a = temporal(ts[0], inner_a, before_b, before_a)
    sib_a, z_a = swap(own_a), halo(own_a)

    weights = (*ws[2], *ws[3])
    inner_b = spatial(spatial_kernel, 7, "spatial_b2")(sc, z_b, own_b, sib_b, *weights)
    before_b = onward(inner_b)
    inner_a = spatial(spatial_kernel, 7, "spatial_a2")(sc, z_a, own_a, sib_a, *weights)
    before_a = onward(inner_a)
    late = temporal(ts[1], inner_b, inner_a, before_b)
    keep, send = call(
        temporal_last_kernel, [pair_shape()] * 2, 5, "temporal_last", moved=1500000
    )(sc, ts[1], inner_a, before_b, before_a, late)
    got = swap(send)
    out = call(
        unpack_kernel, jax.ShapeDtypeStruct((4, C, W), BF16), 2, "unpack", moved=1000000
    )(sc, keep, got)
    return jnp.transpose(out, (0, 2, 1))[None]


def solution(mesh):
    placed = (P("frames", "rows", None, None), P(), P(), P())
    return jax.shard_map(
        on_device,
        mesh=mesh,
        in_specs=placed,
        out_specs=P("frames", "rows", None, None),
        check_vma=False,
    )
```

```python
import functools

import jax
import jax.numpy as jnp
from jax import lax
from jax.experimental import pallas as pl
from jax.experimental.pallas import tpu as pltpu
from jax.sharding import PartitionSpec as P

C = 192
W = 320
PAIR = 2 * W
LANES = 128
EPS = 1e-06
F32 = jnp.float32
BF16 = jnp.bfloat16
VMEM = pl.BlockSpec(memory_space=pltpu.VMEM)
ANY = pl.BlockSpec(memory_space=pl.ANY)
LIMIT = 28 << 20


def call(kernel, outs, n_in, name, scratch=(), flops=0, moved=0, in_specs=None, out_specs=None, aliases=None):
    many = isinstance(outs, (list, tuple))
    if out_specs is None:
        out_specs = [VMEM] * len(outs) if many else VMEM
    return pl.pallas_call(
        kernel,
        out_shape=outs,
        in_specs=in_specs or [VMEM] * n_in,
        out_specs=out_specs,
        scratch_shapes=list(scratch),
        input_output_aliases=aliases or {},
        compiler_params=pltpu.CompilerParams(vmem_limit_bytes=LIMIT),
        cost_estimate=pl.CostEstimate(flops=flops, bytes_accessed=moved, transcendentals=0),
        name=name,
    )


def pair_shape():
    return jax.ShapeDtypeStruct((C, PAIR), BF16)


def core_index():
    return lax.rem(lax.axis_index("frames"), 2)


def weights_kernel(first, sw, g, *outs):
    for k in range(2):
        wt, gt = outs[2 * k : 2 * k + 2]
        for di in range(3):
            for dj in range(3):
                wt[dj * C : (dj + 1) * C, di * C : (di + 1) * C] = sw[first + k, di, dj].T
        gt[...] = jnp.broadcast_to(g[first + k : first + k + 1, :] * 0.5, (LANES, C)).T


def prepare(weights, gains, first):
    shapes = [jax.ShapeDtypeStruct((3 * C, 3 * C), BF16), jax.ShapeDtypeStruct((C, LANES), F32)]
    return call(
        functools.partial(weights_kernel, first), shapes * 2, 2, "weights", moved=3000000
    )(weights, gains)


def taps_kernel(tw, *outs):
    for k in range(2):
        for tap in range(3):
            outs[k][:, tap * C : (tap + 1) * C] = tw[k, tap].T


def prepare_taps(weights):
    shape = jax.ShapeDtypeStruct((C, 3 * C), BF16)
    return call(taps_kernel, [shape] * 2, 1, "taps", moved=1000000)(weights)


def pack_kernel(v, own, sib, rows, sems):
    core = core_index()
    order = (2 * core, 2 * core + 1, 2 - 2 * core, 3 - 2 * core)
    copies = [pltpu.make_async_copy(v.at[order[i]], rows.at[i], sems.at[i]) for i in range(4)]
    for copy in copies:
        copy.start()
    for i, dst in ((0, own), (2, sib)):
        copies[i].wait()
        dst[:, :W] = rows[i]
        copies[i + 1].wait()
        dst[:, W:] = rows[i + 1]


def unpack_rows(x, out, rows, sems, pair):
    copies = []
    for i in range(2):
        rows[i] = x[:, i * W : (i + 1) * W]
        copy = pltpu.make_async_copy(rows.at[i], out.at[2 * pair + i], sems.at[i])
        copy.start()
        copies.append(copy)
    for copy in copies:
        copy.wait()


def unpack_keep_kernel(keep, out, rows, sems):
    unpack_rows(keep, out, rows, sems, core_index())


def unpack_got_kernel(got, part, out, rows, sems):
    del part
    unpack_rows(got, out, rows, sems, 1 - core_index())


def unpack(kernel, x, *part):
    return call(
        kernel,
        jax.ShapeDtypeStruct((4, C, W), BF16),
        1 + len(part),
        "unpack",
        scratch=[pltpu.VMEM((2, C, W), BF16), pltpu.SemaphoreType.DMA((2,))],
        moved=500000,
        in_specs=[VMEM] + [ANY] * len(part),
        out_specs=ANY,
        aliases={1: 0} if part else None,
    )(x, *part)


def tiles_of(x):
    return [x[:, t * LANES : (t + 1) * LANES] for t in range(x.shape[1] // LANES)]


def activate(x, gain, valid):
    x = x.astype(F32)
    scale = lax.rsqrt(jnp.sum(x * x, axis=0, keepdims=True) * (1.0 / C) + EPS)
    if valid is not None:
        scale = scale * valid
    h = x * scale * gain
    return (h + h * jnp.tanh(h)).astype(BF16)


def between(x, y):
    low = lax.broadcasted_iota(jnp.int32, (1, LANES), 1) < LANES // 2
    turned = [pltpu.roll(t, LANES // 2, 1) for t in x[2:] + y[:3]]
    return [jnp.where(low, turned[i], turned[i + 1]) for i in range(5)]


def stack(rows, at, x, y):
    for t, (above, middle, below) in enumerate(zip(x, between(x, y), y)):
        lanes = slice(at + t * LANES, at + (t + 1) * LANES)
        rows[:C, lanes] = above
        rows[C : 2 * C, lanes] = middle
        rows[2 * C :, lanes] = below


def convolved(weight, rows):
    lane = lax.broadcasted_iota(jnp.int32, (1, LANES), 1)
    out = []
    for at in range(0, rows.shape[1], PAIR):
        product = jnp.dot(weight[...], rows[:, at : at + PAIR], preferred_element_type=F32)
        left, middle, right = (tiles_of(product[dj * C : (dj + 1) * C]) for dj in range(3))
        left = [pltpu.roll(t, 1, 1) for t in left]
        right = [pltpu.roll(t, LANES - 1, 1) for t in right]
        for t in range(5):
            a = jnp.where(lane == 0, left[t - 1] if t else 0.0, left[t])
            b = jnp.where(lane == LANES - 1, right[t + 1] if t < 4 else 0.0, right[t])
            if t == W // LANES:
                a = jnp.where(lane == W % LANES, 0.0, a)
                b = jnp.where(lane == W % LANES - 1, 0.0, b)
            out.append(middle[t] + a + b)
    return out


def spatial_body(z, own, sib, w1, g1, w2, g2, out, s1, s2):
    core, row = core_index(), lax.axis_index("rows")
    is0 = core == 0
    top = is0 & (row == 0)
    bottom = (core == 1) & (row == lax.axis_size("rows") - 1)
    gain = g1[...]
    above, mid, below = [], [], []
    for tz, to, ts in zip(z, own, sib):
        above.append(activate(jnp.where(is0, tz, ts), gain, None))
        mid.append(activate(to, gain, None))
        below.append(activate(jnp.where(is0, ts, tz), gain, None))
    stack(s1, 0, above, mid)
    stack(s1, PAIR, mid, below)
    lane = lax.broadcasted_iota(jnp.int32, (1, LANES), 1)
    gain = g2[...]
    act = []
    for t, x in enumerate(convolved(w1, s1)):
        pixel = lane + t * LANES
        outside = ((pixel < W) & top) | ((pixel >= 3 * W) & bottom)
        act.append(activate(x.astype(BF16), gain, jnp.where(outside, 0.0, 1.0).astype(F32)))
    stack(s2, 0, act[:5], act[5:])
    for t, (x, y) in enumerate(zip(own, convolved(w2, s2))):
        out[:, t * LANES : (t + 1) * LANES] = (x.astype(F32) + y).astype(BF16)


def spatial_kernel(z, own, sib, *rest):
    spatial_body(tiles_of(z), tiles_of(own), tiles_of(sib), *rest)


def spatial_pick_kernel(pick, z0, own0, sib0, z1, own1, sib1, *rest):
    mine = core_index() == pick

    def chosen(x, y):
        return [jnp.where(mine, s, t) for s, t in zip(tiles_of(x), tiles_of(y))]

    spatial_body(chosen(z0, z1), chosen(own0, own1), chosen(sib0, sib1), *rest)


def spatial(kernel, n_in, name):
    return call(
        kernel,
        pair_shape(),
        n_in,
        name,
        scratch=[pltpu.VMEM((3 * C, 2 * PAIR), BF16), pltpu.VMEM((3 * C, PAIR), BF16)],
        flops=2 * C * C * 9 * 3 * PAIR,
        moved=4000000,
    )


def mixed(wt, x0, x1, x2):
    total = x0[...].astype(F32)
    for tap, x in enumerate((x0, x1, x2)):
        total = total + jnp.dot(
            wt[:, tap * C : (tap + 1) * C], x[...], preferred_element_type=F32
        )
    return total.astype(BF16)


def temporal_kernel(wt, x0, x1, x2, out):
    out[...] = mixed(wt, x0, x1, x2)


def temporal(wt, x0, x1, x2):
    return call(
        temporal_kernel, pair_shape(), 4, "temporal", flops=2 * C * C * 3 * PAIR, moved=1300000
    )(wt, x0, x1, x2)


def temporal_last_kernel(wt, x0, x1, x2, late, keep, send):
    early = mixed(wt, x0, x1, x2)
    is0 = core_index() == 0
    other = late[...]
    keep[...] = jnp.where(is0, early, other)
    send[...] = jnp.where(is0, other, early)


def on_device(video, spatial_weights, norm_gains, temporal_weights):
    frames, rows = lax.axis_size("frames"), lax.axis_size("rows")
    swaps = [(i, i ^ 1) for i in range(frames)]
    across = []
    for f in range(frames):
        for r in range(rows):
            to = r + 1 if f % 2 else r - 1
            if 0 <= to < rows:
                across.append((f * rows + r, (f ^ 1) * rows + to))
    later = [(i, i + 2) for i in range(frames - 2)]

    def swap(x):
        return lax.ppermute(x, "frames", swaps)

    def halo(x):
        return lax.ppermute(x, ("frames", "rows"), across)

    def onward(x):
        return lax.ppermute(x, "frames", later)

    view = jnp.transpose(video[0], (0, 2, 1))
    own_m, sib_m = call(
        pack_kernel,
        [pair_shape()] * 2,
        1,
        "pack",
        scratch=[pltpu.VMEM((4, C, W), BF16), pltpu.SemaphoreType.DMA((4,))],
        moved=1000000,
        in_specs=[pl.BlockSpec(memory_space=pltpu.HBM)],
    )(view)
    own_o = swap(sib_m)
    sib_o = swap(own_m)
    z_o = halo(own_m)
    z_m = halo(own_o)
    ts = prepare_taps(temporal_weights)
    ws = [prepare(spatial_weights, norm_gains, 2 * k) for k in range(2)]

    arrays = (z_m, own_m, sib_m, z_o, own_o, sib_o)
    inner_b = spatial(functools.partial(spatial_pick_kernel, 1), 10, "spatial_b")(*arrays, *ws[0])
    before_b = onward(inner_b)
    inner_a = spatial(functools.partial(spatial_pick_kernel, 0), 10, "spatial_a")(*arrays, *ws[0])
    before_a = onward(inner_a)
    own_b = temporal(ts[0], inner_b, inner_a, before_b)
    sib_b, z_b = swap(own_b), halo(own_b)
    own_a = temporal(ts[0], inner_a, before_b, before_a)
    sib_a, z_a = swap(own_a), halo(own_a)

    inner_b = spatial(spatial_kernel, 7, "spatial_b2")(z_b, own_b, sib_b, *ws[1])
    before_b = onward(inner_b)
    inner_a = spatial(spatial_kernel, 7, "spatial_a2")(z_a, own_a, sib_a, *ws[1])
    before_a = onward(inner_a)
    late = temporal(ts[1], inner_b, inner_a, before_b)
    keep, send = call(temporal_last_kernel, [pair_shape()] * 2, 5, "temporal_last", moved=1500000)(
        ts[1], inner_a, before_b, before_a, late
    )
    got = swap(send)
    out = unpack(unpack_got_kernel, got, unpack(unpack_keep_kernel, keep))
    return jnp.transpose(out, (0, 2, 1))[None]


def solution(mesh):
    placed = (P("frames", "rows", None, None), P(), P(), P())
    return jax.shard_map(
        on_device,
        mesh=mesh,
        in_specs=placed,
        out_specs=P("frames", "rows", None, None),
        check_vma=False,
    )
```

```python
import functools

import jax
import jax.numpy as jnp
from jax import lax
from jax.experimental import pallas as pl
from jax.experimental.pallas import tpu as pltpu
from jax.sharding import PartitionSpec as P

C = 192
W = 320
PAIR = 2 * W
LANES = 128
EPS = 1e-06
F32 = jnp.float32
BF16 = jnp.bfloat16
VMEM = pl.BlockSpec(memory_space=pltpu.VMEM)
ANY = pl.BlockSpec(memory_space=pl.ANY)
LIMIT = 20 << 20


def call(kernel, outs, n_in, name, scratch=(), flops=0, moved=0, in_specs=None, out_specs=None, aliases=None):
    many = isinstance(outs, (list, tuple))
    if out_specs is None:
        out_specs = [VMEM] * len(outs) if many else VMEM
    return pl.pallas_call(
        kernel,
        out_shape=outs,
        in_specs=in_specs or [VMEM] * n_in,
        out_specs=out_specs,
        scratch_shapes=list(scratch),
        input_output_aliases=aliases or {},
        compiler_params=pltpu.CompilerParams(vmem_limit_bytes=LIMIT),
        cost_estimate=pl.CostEstimate(flops=flops, bytes_accessed=moved, transcendentals=0),
        name=name,
    )


def pair_shape():
    return jax.ShapeDtypeStruct((C, PAIR), BF16)


def core_index():
    return lax.rem(lax.axis_index("frames"), 2)


def weights_kernel(sw, g, tw, w0, w1, w2, w3, g0, g1, g2, g3, t0, t1, held, sems, taps, tap_sems):
    copies = [
        pltpu.make_async_copy(sw.at[k, di], held.at[k, di], sems.at[k, di]) for k in range(4) for di in range(3)
    ]
    tap_copies = [pltpu.make_async_copy(tw.at[b], taps.at[b], tap_sems.at[b]) for b in range(2)]
    for copy in copies + tap_copies:
        copy.start()
    for k, gt in enumerate((g0, g1, g2, g3)):
        gt[...] = jnp.broadcast_to(g[k : k + 1, :] * 0.5, (LANES, C)).T
    for k, wt in enumerate((w0, w1, w2, w3)):
        for di in range(3):
            copies[3 * k + di].wait()
            for dj in range(3):
                wt[dj * C : (dj + 1) * C, di * C : (di + 1) * C] = held[k, di, dj].T
    for b, wt in enumerate((t0, t1)):
        tap_copies[b].wait()
        for tap in range(3):
            wt[:, tap * C : (tap + 1) * C] = taps[b, tap].T


def in_hbm(x):
    return pltpu.with_memory_space_constraint(x, pltpu.HBM)


def prepare(weights, gains, taps):
    shape = jax.ShapeDtypeStruct
    outs = call(
        weights_kernel,
        [shape((3 * C, 3 * C), BF16)] * 4 + [shape((C, LANES), F32)] * 4 + [shape((C, 3 * C), BF16)] * 2,
        3,
        "weights",
        scratch=[
            pltpu.VMEM((4, 3, 3, C, C), BF16),
            pltpu.SemaphoreType.DMA((4, 3)),
            pltpu.VMEM((2, 3, C, C), BF16),
            pltpu.SemaphoreType.DMA((2,)),
        ],
        moved=8000000,
        in_specs=[ANY, VMEM, ANY],
    )(in_hbm(weights), gains, in_hbm(taps))
    return outs[:4], outs[4:8], outs[8:]


def pack_kernel(v, both, rows, sems):
    core = core_index()
    order = (2 - 2 * core, 3 - 2 * core, 2 * core, 2 * core + 1)
    copies = [pltpu.make_async_copy(v.at[order[i]], rows.at[i], sems.at[i]) for i in range(4)]
    for copy in copies:
        copy.start()
    for i in range(4):
        copies[i].wait()
        both[i // 2, :, (i % 2) * W : (i % 2 + 1) * W] = rows[i]


def join_kernel(mine, other, owned):
    owned[0] = mine[1]
    owned[1] = other[0]


def unpack_rows(x, out, rows, sems, pair):
    copies = []
    for i in range(2):
        rows[i] = x[:, i * W : (i + 1) * W]
        copy = pltpu.make_async_copy(rows.at[i], out.at[2 * pair + i], sems.at[i])
        copy.start()
        copies.append(copy)
    for copy in copies:
        copy.wait()


def unpack_keep_kernel(keep, out, rows, sems):
    unpack_rows(keep, out, rows, sems, core_index())


def unpack_got_kernel(got, part, out, rows, sems):
    del part
    unpack_rows(got, out, rows, sems, 1 - core_index())


def unpack(kernel, x, *part):
    return call(
        kernel,
        jax.ShapeDtypeStruct((4, C, W), BF16),
        1 + len(part),
        "unpack",
        scratch=[pltpu.VMEM((2, C, W), BF16), pltpu.SemaphoreType.DMA((2,))],
        moved=500000,
        in_specs=[VMEM] + [ANY] * len(part),
        out_specs=ANY,
        aliases={1: 0} if part else None,
    )(x, *part)


def tiles_of(x):
    return [x[:, t * LANES : (t + 1) * LANES] for t in range(x.shape[1] // LANES)]


def activate(x, gain, valid):
    x = x.astype(F32)
    scale = lax.rsqrt(jnp.sum(x * x, axis=0, keepdims=True) * (1.0 / C) + EPS)
    if valid is not None:
        scale = scale * valid
    h = x * scale * gain
    return (h + h * jnp.tanh(h)).astype(BF16)


def between(x, y):
    low = lax.broadcasted_iota(jnp.int32, (1, LANES), 1) < LANES // 2
    turned = [pltpu.roll(t, LANES // 2, 1) for t in x[2:] + y[:3]]
    return [jnp.where(low, turned[i], turned[i + 1]) for i in range(5)]


def stack(rows, at, x, y):
    for t, (above, middle, below) in enumerate(zip(x, between(x, y), y)):
        lanes = slice(at + t * LANES, at + (t + 1) * LANES)
        rows[:C, lanes] = above
        rows[C : 2 * C, lanes] = middle
        rows[2 * C :, lanes] = below


def convolved(weight, rows):
    lane = lax.broadcasted_iota(jnp.int32, (1, LANES), 1)
    out = []
    for at in range(0, rows.shape[1], PAIR):
        product = jnp.dot(weight[...], rows[:, at : at + PAIR], preferred_element_type=F32)
        left, middle, right = (tiles_of(product[dj * C : (dj + 1) * C]) for dj in range(3))
        left = [pltpu.roll(t, 1, 1) for t in left]
        right = [pltpu.roll(t, LANES - 1, 1) for t in right]
        for t in range(5):
            a = jnp.where(lane == 0, left[t - 1] if t else 0.0, left[t])
            b = jnp.where(lane == LANES - 1, right[t + 1] if t < 4 else 0.0, right[t])
            if t == W // LANES:
                a = jnp.where(lane == W % LANES, 0.0, a)
                b = jnp.where(lane == W % LANES - 1, 0.0, b)
            out.append(middle[t] + a + b)
    return out


def either(first, x, y):
    return [jnp.where(first, s, t) for s, t in zip(x, y)]


def near_body(own, sib, w1, g1, g2, act1, act2, s1):
    is0 = core_index() == 0
    gain = g1[...]
    own = [activate(t, gain, None) for t in own]
    sib = [activate(t, gain, None) for t in sib]
    stack(s1, 0, either(is0, own, sib), either(is0, sib, own))
    gain = g2[...]
    for t, x in enumerate(convolved(w1, s1)):
        lanes = slice(t * LANES, (t + 1) * LANES)
        act1[:, lanes] = own[t]
        act2[:, lanes] = activate(x.astype(BF16), gain, None)


def near_mine_kernel(mine, *rest):
    near_body(tiles_of(mine.at[1]), tiles_of(mine.at[0]), *rest)


def near_other_kernel(other, *rest):
    near_body(tiles_of(other.at[0]), tiles_of(other.at[1]), *rest)


def near(kernel, arrays, w1, g1, g2):
    return call(
        kernel,
        [pair_shape()] * 2,
        len(arrays) + 3,
        "near",
        scratch=[pltpu.VMEM((3 * C, PAIR), BF16)],
        flops=2 * C * C * 9 * PAIR,
        moved=2000000,
    )(*arrays, w1, g1, g2)


def far_body(z, own, act1, act2, w1, g1, w2, g2, out, s1, s2):
    core, row = core_index(), lax.axis_index("rows")
    is0 = core == 0
    top = is0 & (row == 0)
    bottom = (core == 1) & (row == lax.axis_size("rows") - 1)
    gain = g1[...]
    z = [activate(t, gain, None) for t in z]
    stack(s1, 0, either(is0, z, act1), either(is0, act1, z))
    lane = lax.broadcasted_iota(jnp.int32, (1, LANES), 1)
    gain = g2[...]
    far = []
    for t, x in enumerate(convolved(w1, s1)):
        pixel = lane + t * LANES
        outside = ((pixel < W) & top) | ((pixel >= W) & bottom)
        far.append(activate(x.astype(BF16), gain, jnp.where(outside, 0.0, 1.0).astype(F32)))
    stack(s2, 0, either(is0, far, act2), either(is0, act2, far))
    for t, (x, y) in enumerate(zip(own, convolved(w2, s2))):
        out[:, t * LANES : (t + 1) * LANES] = (x.astype(F32) + y).astype(BF16)


def far_pick_kernel(pick, z, mine, other, act1_m, act2_m, act1_o, act2_o, *rest):
    is_mine = core_index() == pick

    def chosen(x, y):
        return either(is_mine, tiles_of(x), tiles_of(y))

    far_body(
        chosen(z.at[1], z.at[0]),
        chosen(mine.at[1], other.at[0]),
        chosen(act1_m, act1_o),
        chosen(act2_m, act2_o),
        *rest,
    )


def far(kernel, arrays, w1, g1, w2, g2):
    return call(
        kernel,
        pair_shape(),
        len(arrays) + 4,
        "far",
        scratch=[pltpu.VMEM((3 * C, PAIR), BF16)] * 2,
        flops=2 * C * C * 9 * 2 * PAIR,
        moved=4000000,
    )(*arrays, w1, g1, w2, g2)


def spatial_body(z, own, sib, w1, g1, w2, g2, out, s1, s2):
    core, row = core_index(), lax.axis_index("rows")
    is0 = core == 0
    top = is0 & (row == 0)
    bottom = (core == 1) & (row == lax.axis_size("rows") - 1)
    gain = g1[...]
    above, mid, below = [], [], []
    for tz, to, ts in zip(z, own, sib):
        above.append(activate(jnp.where(is0, tz, ts), gain, None))
        mid.append(activate(to, gain, None))
        below.append(activate(jnp.where(is0, ts, tz), gain, None))
    stack(s1, 0, above, mid)
    stack(s1, PAIR, mid, below)
    lane = lax.broadcasted_iota(jnp.int32, (1, LANES), 1)
    gain = g2[...]
    act = []
    for t, x in enumerate(convolved(w1, s1)):
        pixel = lane + t * LANES
        outside = ((pixel < W) & top) | ((pixel >= 3 * W) & bottom)
        act.append(activate(x.astype(BF16), gain, jnp.where(outside, 0.0, 1.0).astype(F32)))
    stack(s2, 0, act[:5], act[5:])
    for t, (x, y) in enumerate(zip(own, convolved(w2, s2))):
        out[:, t * LANES : (t + 1) * LANES] = (x.astype(F32) + y).astype(BF16)


def spatial_kernel(z, own, sib, *rest):
    spatial_body(tiles_of(z), tiles_of(own), tiles_of(sib), *rest)


def spatial(kernel, n_in, name):
    return call(
        kernel,
        pair_shape(),
        n_in,
        name,
        scratch=[pltpu.VMEM((3 * C, 2 * PAIR), BF16), pltpu.VMEM((3 * C, PAIR), BF16)],
        flops=2 * C * C * 9 * 3 * PAIR,
        moved=4000000,
    )


def mixed(wt, x0, x1, x2):
    total = x0[...].astype(F32)
    for tap, x in enumerate((x0, x1, x2)):
        total = total + jnp.dot(
            wt[:, tap * C : (tap + 1) * C], x[...], preferred_element_type=F32
        )
    return total.astype(BF16)


def temporal_kernel(wt, x0, x1, x2, out):
    out[...] = mixed(wt, x0, x1, x2)


def temporal(wt, x0, x1, x2):
    return call(
        temporal_kernel, pair_shape(), 4, "temporal", flops=2 * C * C * 3 * PAIR, moved=1300000
    )(wt, x0, x1, x2)


def temporal_last_kernel(wt, x0, x1, x2, late, keep, send):
    early = mixed(wt, x0, x1, x2)
    is0 = core_index() == 0
    other = late[...]
    keep[...] = jnp.where(is0, early, other)
    send[...] = jnp.where(is0, other, early)


def on_device(video, spatial_weights, norm_gains, temporal_weights):
    frames, rows = lax.axis_size("frames"), lax.axis_size("rows")
    swaps = [(i, i ^ 1) for i in range(frames)]
    across = []
    for f in range(frames):
        for r in range(rows):
            to = r + 1 if f % 2 else r - 1
            if 0 <= to < rows:
                across.append((f * rows + r, (f ^ 1) * rows + to))
    later = [(i, i + 2) for i in range(frames - 2)]

    def swap(x):
        return lax.ppermute(x, "frames", swaps)

    def halo(x):
        return lax.ppermute(x, ("frames", "rows"), across)

    def onward(x):
        return lax.ppermute(x, "frames", later)

    view = in_hbm(jnp.transpose(video[0], (0, 2, 1)))
    mine = call(
        pack_kernel,
        jax.ShapeDtypeStruct((2, C, PAIR), BF16),
        1,
        "pack",
        scratch=[pltpu.VMEM((4, C, W), BF16), pltpu.SemaphoreType.DMA((4,))],
        moved=1000000,
        in_specs=[ANY],
    )(view)
    other = swap(mine)
    owned = call(join_kernel, jax.ShapeDtypeStruct((2, C, PAIR), BF16), 2, "join", moved=1000000)(mine, other)
    z = halo(owned)
    ws, gs, ts = prepare(spatial_weights, norm_gains, temporal_weights)

    first, both = (ws[0], gs[0], gs[1]), (ws[0], gs[0], ws[1], gs[1])
    arrays = (z, mine, other, *near(near_mine_kernel, (mine,), *first), *near(near_other_kernel, (other,), *first))
    inner_b = far(functools.partial(far_pick_kernel, 1), arrays, *both)
    before_b = onward(inner_b)
    inner_a = far(functools.partial(far_pick_kernel, 0), arrays, *both)
    before_a = onward(inner_a)

    own_b = temporal(ts[0], inner_b, inner_a, before_b)
    sib_b, z_b = swap(own_b), halo(own_b)
    own_a = temporal(ts[0], inner_a, before_b, before_a)
    sib_a, z_a = swap(own_a), halo(own_a)
    both = (ws[2], gs[2], ws[3], gs[3])
    inner_b = spatial(spatial_kernel, 7, "spatial_b")(z_b, own_b, sib_b, *both)
    before_b = onward(inner_b)
    inner_a = spatial(spatial_kernel, 7, "spatial_a")(z_a, own_a, sib_a, *both)
    before_a = onward(inner_a)
    late = temporal(ts[1], inner_b, inner_a, before_b)
    keep, send = call(temporal_last_kernel, [pair_shape()] * 2, 5, "temporal_last", moved=1500000)(
        ts[1], inner_a, before_b, before_a, late
    )
    got = swap(send)
    out = unpack(unpack_got_kernel, got, unpack(unpack_keep_kernel, keep))
    return jnp.transpose(out, (0, 2, 1))[None]


def solution(mesh):
    placed = (P("frames", "rows", None, None), P(), P(), P())
    return jax.shard_map(
        on_device,
        mesh=mesh,
        in_specs=placed,
        out_specs=P("frames", "rows", None, None),
        check_vma=False,
    )
```

```python
import functools

import jax
import jax.numpy as jnp
from jax import lax
from jax.experimental import pallas as pl
from jax.experimental.pallas import tpu as pltpu
from jax.sharding import PartitionSpec as P

C = 192
W = 320
PAIR = 2 * W
LANES = 128
EPS = 1e-06
F32 = jnp.float32
BF16 = jnp.bfloat16
VMEM = pl.BlockSpec(memory_space=pltpu.VMEM)
ANY = pl.BlockSpec(memory_space=pl.ANY)
LIMIT = 20 << 20


def call(kernel, outs, n_in, name, scratch=(), flops=0, moved=0, in_specs=None, out_specs=None, aliases=None):
    many = isinstance(outs, (list, tuple))
    if out_specs is None:
        out_specs = [VMEM] * len(outs) if many else VMEM
    return pl.pallas_call(
        kernel,
        out_shape=outs,
        in_specs=in_specs or [VMEM] * n_in,
        out_specs=out_specs,
        scratch_shapes=list(scratch),
        input_output_aliases=aliases or {},
        compiler_params=pltpu.CompilerParams(vmem_limit_bytes=LIMIT),
        cost_estimate=pl.CostEstimate(flops=flops, bytes_accessed=moved, transcendentals=0),
        name=name,
    )


def pair_shape():
    return jax.ShapeDtypeStruct((C, PAIR), BF16)


def core_index():
    return lax.rem(lax.axis_index("frames"), 2)


def gain_column(g, k):
    return jnp.broadcast_to(g[k : k + 1, :] * 0.5, (LANES, C)).T


def transpose_taps(source, wt):
    for di in range(3):
        for dj in range(3):
            wt[dj * C : (dj + 1) * C, di * C : (di + 1) * C] = source[di, dj].T


def weights_kernel(sw, g, tw, w0, w1, w2, w3, g0, g1, g2, g3, t0, t1, held, taps, gains, sems, more_sems):
    gain_copy = pltpu.make_async_copy(g, gains, more_sems.at[0])
    tap_copy = pltpu.make_async_copy(tw, taps, more_sems.at[1])
    copies = [pltpu.make_async_copy(sw.at[k], held.at[k], sems.at[k]) for k in range(4)]
    gain_copy.start()
    for copy in copies:
        copy.start()
    tap_copy.start()
    gain_copy.wait()
    for k, gt in enumerate((g0, g1, g2, g3)):
        gt[...] = gain_column(gains, k)
    for k, wt in enumerate((w0, w1, w2, w3)):
        copies[k].wait()
        transpose_taps(held.at[k], wt)
    tap_copy.wait()
    for b, wt in enumerate((t0, t1)):
        for tap in range(3):
            wt[:, tap * C : (tap + 1) * C] = taps[b, tap].T


def in_hbm(x):
    return pltpu.with_memory_space_constraint(x, pltpu.HBM)


def prepare(weights, gains, taps):
    shape = jax.ShapeDtypeStruct
    outs = call(
        weights_kernel,
        [shape((3 * C, 3 * C), BF16)] * 4 + [shape((C, LANES), F32)] * 4 + [shape((C, 3 * C), BF16)] * 2,
        3,
        "weights",
        scratch=[
            pltpu.VMEM((4, 3, 3, C, C), BF16),
            pltpu.VMEM((2, 3, C, C), BF16),
            pltpu.VMEM((4, C), F32),
            pltpu.SemaphoreType.DMA((4,)),
            pltpu.SemaphoreType.DMA((2,)),
        ],
        moved=6000000,
        in_specs=[ANY] * 3,
    )(in_hbm(weights), in_hbm(gains), in_hbm(taps))
    return outs[:4], outs[4:8], outs[8:]


def pack_kernel(v, both, rows, sems):
    core = core_index()
    order = (2 - 2 * core, 3 - 2 * core, 2 * core, 2 * core + 1)
    copies = [pltpu.make_async_copy(v.at[order[i]], rows.at[i], sems.at[i]) for i in range(4)]
    for copy in copies:
        copy.start()
    for i in range(4):
        copies[i].wait()
        both[i // 2, :, (i % 2) * W : (i % 2 + 1) * W] = rows[i]


def join_kernel(mine, other, owned):
    owned[0] = mine[1]
    owned[1] = other[0]


def unpack_rows(x, out, rows, sems, pair):
    copies = []
    for i in range(2):
        rows[i] = x[:, i * W : (i + 1) * W]
        copy = pltpu.make_async_copy(rows.at[i], out.at[2 * pair + i], sems.at[i])
        copy.start()
        copies.append(copy)
    for copy in copies:
        copy.wait()


def unpack_keep_kernel(keep, out, rows, sems):
    unpack_rows(keep, out, rows, sems, core_index())


def unpack_got_kernel(got, part, out, rows, sems):
    del part
    unpack_rows(got, out, rows, sems, 1 - core_index())


def unpack(kernel, x, *part):
    return call(
        kernel,
        jax.ShapeDtypeStruct((4, C, W), BF16),
        1 + len(part),
        "unpack",
        scratch=[pltpu.VMEM((2, C, W), BF16), pltpu.SemaphoreType.DMA((2,))],
        moved=500000,
        in_specs=[VMEM] + [ANY] * len(part),
        out_specs=ANY,
        aliases={1: 0} if part else None,
    )(x, *part)


def tiles_of(x):
    return [x[:, t * LANES : (t + 1) * LANES] for t in range(x.shape[1] // LANES)]


def activate(x, gain, valid):
    x = x.astype(F32)
    scale = lax.rsqrt(jnp.sum(x * x, axis=0, keepdims=True) * (1.0 / C) + EPS)
    if valid is not None:
        scale = scale * valid
    h = x * scale * gain
    return (h + h * jnp.tanh(h)).astype(BF16)


def between(x, y):
    low = lax.broadcasted_iota(jnp.int32, (1, LANES), 1) < LANES // 2
    turned = [pltpu.roll(t, LANES // 2, 1) for t in x[2:] + y[:3]]
    return [jnp.where(low, turned[i], turned[i + 1]) for i in range(5)]


def stack(rows, at, x, y):
    for t, (above, middle, below) in enumerate(zip(x, between(x, y), y)):
        lanes = slice(at + t * LANES, at + (t + 1) * LANES)
        rows[:C, lanes] = above
        rows[C : 2 * C, lanes] = middle
        rows[2 * C :, lanes] = below


def convolved(weight, rows):
    lane = lax.broadcasted_iota(jnp.int32, (1, LANES), 1)
    out = []
    for at in range(0, rows.shape[1], PAIR):
        product = jnp.dot(weight[...], rows[:, at : at + PAIR], preferred_element_type=F32)
        left, middle, right = (tiles_of(product[dj * C : (dj + 1) * C]) for dj in range(3))
        left = [pltpu.roll(t, 1, 1) for t in left]
        right = [pltpu.roll(t, LANES - 1, 1) for t in right]
        for t in range(5):
            a = jnp.where(lane == 0, left[t - 1] if t else 0.0, left[t])
            b = jnp.where(lane == LANES - 1, right[t + 1] if t < 4 else 0.0, right[t])
            if t == W // LANES:
                a = jnp.where(lane == W % LANES, 0.0, a)
                b = jnp.where(lane == W % LANES - 1, 0.0, b)
            out.append(middle[t] + a + b)
    return out


def either(first, x, y):
    return [jnp.where(first, s, t) for s, t in zip(x, y)]


def near_body(own, sib, w1, g1, g2, act1, act2, s1):
    is0 = core_index() == 0
    gain = g1[...]
    own = [activate(t, gain, None) for t in own]
    sib = [activate(t, gain, None) for t in sib]
    stack(s1, 0, either(is0, own, sib), either(is0, sib, own))
    gain = g2[...]
    for t, x in enumerate(convolved(w1, s1)):
        lanes = slice(t * LANES, (t + 1) * LANES)
        act1[:, lanes] = own[t]
        act2[:, lanes] = activate(x.astype(BF16), gain, None)


def near_kernel(which, pairs, *rest):
    near_body(tiles_of(pairs.at[which]), tiles_of(pairs.at[1 - which]), *rest)


def near(which, pairs, w1, g1, g2):
    return call(
        functools.partial(near_kernel, which),
        [pair_shape()] * 2,
        4,
        "near",
        scratch=[pltpu.VMEM((3 * C, PAIR), BF16)],
        flops=2 * C * C * 9 * PAIR,
        moved=2000000,
    )(pairs, w1, g1, g2)


def far_body(z, own, act1, act2, w1, g1, w2, g2, out, s1, s2):
    core, row = core_index(), lax.axis_index("rows")
    is0 = core == 0
    top = is0 & (row == 0)
    bottom = (core == 1) & (row == lax.axis_size("rows") - 1)
    gain = g1[...]
    z = [activate(t, gain, None) for t in z]
    stack(s1, 0, either(is0, z, act1), either(is0, act1, z))
    lane = lax.broadcasted_iota(jnp.int32, (1, LANES), 1)
    gain = g2[...]
    far = []
    for t, x in enumerate(convolved(w1, s1)):
        pixel = lane + t * LANES
        outside = ((pixel < W) & top) | ((pixel >= W) & bottom)
        far.append(activate(x.astype(BF16), gain, jnp.where(outside, 0.0, 1.0).astype(F32)))
    stack(s2, 0, either(is0, far, act2), either(is0, act2, far))
    for t, (x, y) in enumerate(zip(own, convolved(w2, s2))):
        out[:, t * LANES : (t + 1) * LANES] = (x.astype(F32) + y).astype(BF16)


def far_pick_kernel(pick, z, owned, act1_m, act2_m, act1_o, act2_o, *rest):
    is_mine = core_index() == pick

    def chosen(x, y):
        return either(is_mine, tiles_of(x), tiles_of(y))

    far_body(
        chosen(z.at[1], z.at[0]),
        chosen(owned.at[0], owned.at[1]),
        chosen(act1_m, act1_o),
        chosen(act2_m, act2_o),
        *rest,
    )


def far(kernel, arrays, w1, g1, w2, g2):
    return call(
        kernel,
        pair_shape(),
        len(arrays) + 4,
        "far",
        scratch=[pltpu.VMEM((3 * C, PAIR), BF16)] * 2,
        flops=2 * C * C * 9 * 2 * PAIR,
        moved=4000000,
    )(*arrays, w1, g1, w2, g2)


def spatial_body(z, own, sib, w1, g1, w2, g2, out, s1, s2):
    core, row = core_index(), lax.axis_index("rows")
    is0 = core == 0
    top = is0 & (row == 0)
    bottom = (core == 1) & (row == lax.axis_size("rows") - 1)
    gain = g1[...]
    above, mid, below = [], [], []
    for tz, to, ts in zip(z, own, sib):
        above.append(activate(jnp.where(is0, tz, ts), gain, None))
        mid.append(activate(to, gain, None))
        below.append(activate(jnp.where(is0, ts, tz), gain, None))
    stack(s1, 0, above, mid)
    stack(s1, PAIR, mid, below)
    lane = lax.broadcasted_iota(jnp.int32, (1, LANES), 1)
    gain = g2[...]
    act = []
    for t, x in enumerate(convolved(w1, s1)):
        pixel = lane + t * LANES
        outside = ((pixel < W) & top) | ((pixel >= 3 * W) & bottom)
        act.append(activate(x.astype(BF16), gain, jnp.where(outside, 0.0, 1.0).astype(F32)))
    stack(s2, 0, act[:5], act[5:])
    for t, (x, y) in enumerate(zip(own, convolved(w2, s2))):
        out[:, t * LANES : (t + 1) * LANES] = (x.astype(F32) + y).astype(BF16)


def spatial_kernel(z, own, sib, *rest):
    spatial_body(tiles_of(z), tiles_of(own), tiles_of(sib), *rest)


def spatial(kernel, n_in, name):
    return call(
        kernel,
        pair_shape(),
        n_in,
        name,
        scratch=[pltpu.VMEM((3 * C, 2 * PAIR), BF16), pltpu.VMEM((3 * C, PAIR), BF16)],
        flops=2 * C * C * 9 * 3 * PAIR,
        moved=4000000,
    )


def mixed(wt, x0, x1, x2):
    total = x0[...].astype(F32)
    for tap, x in enumerate((x0, x1, x2)):
        total = total + jnp.dot(
            wt[:, tap * C : (tap + 1) * C], x[...], preferred_element_type=F32
        )
    return total.astype(BF16)


def temporal_kernel(wt, x0, x1, x2, out):
    out[...] = mixed(wt, x0, x1, x2)


def temporal(wt, x0, x1, x2):
    return call(
        temporal_kernel, pair_shape(), 4, "temporal", flops=2 * C * C * 3 * PAIR, moved=1300000
    )(wt, x0, x1, x2)


def temporal_late_kernel(wt, x0, x1, x2, y0, out, part):
    out[...] = mixed(wt, x0, x1, x2)
    total = y0[...].astype(F32)
    for tap, y in enumerate((y0, x2)):
        total = total + jnp.dot(
            wt[:, tap * C : (tap + 1) * C], y[...], preferred_element_type=F32
        )
    part[...] = total


def temporal_last_kernel(wt, part, y2, late, keep, send):
    early = part[...] + jnp.dot(wt[:, 2 * C :], y2[...], preferred_element_type=F32)
    early = early.astype(BF16)
    is0 = core_index() == 0
    other = late[...]
    keep[...] = jnp.where(is0, early, other)
    send[...] = jnp.where(is0, other, early)


def on_device(video, spatial_weights, norm_gains, temporal_weights):
    frames, rows = lax.axis_size("frames"), lax.axis_size("rows")
    swaps = [(i, i ^ 1) for i in range(frames)]
    across = []
    for f in range(frames):
        for r in range(rows):
            to = r + 1 if f % 2 else r - 1
            if 0 <= to < rows:
                across.append((f * rows + r, (f ^ 1) * rows + to))
    later = [(i, i + 2) for i in range(frames - 2)]

    def swap(x):
        return lax.ppermute(x, "frames", swaps)

    def halo(x):
        return lax.ppermute(x, ("frames", "rows"), across)

    def onward(x):
        return lax.ppermute(x, "frames", later)

    view = in_hbm(jnp.transpose(video[0], (0, 2, 1)))
    mine = call(
        pack_kernel,
        jax.ShapeDtypeStruct((2, C, PAIR), BF16),
        1,
        "pack",
        scratch=[pltpu.VMEM((4, C, W), BF16), pltpu.SemaphoreType.DMA((4,))],
        moved=1000000,
        in_specs=[ANY],
    )(view)
    other = swap(mine)
    owned = call(join_kernel, jax.ShapeDtypeStruct((2, C, PAIR), BF16), 2, "join", moved=1000)(mine, other)
    z = halo(owned)
    (w0, w1, w2, w3), (g0, g1, g2, g3), ts = prepare(spatial_weights, norm_gains, temporal_weights)

    near_m = near(1, mine, w0, g0, g1)
    near_o = near(0, other, w0, g0, g1)
    arrays = (z, owned, *near_m, *near_o)
    inner_b = far(functools.partial(far_pick_kernel, 1), arrays, w0, g0, w1, g1)
    before_b = onward(inner_b)
    inner_a = far(functools.partial(far_pick_kernel, 0), arrays, w0, g0, w1, g1)
    before_a = onward(inner_a)

    own_b = temporal(ts[0], inner_b, inner_a, before_b)
    z_b, sib_b = halo(own_b), swap(own_b)
    own_a = temporal(ts[0], inner_a, before_b, before_a)
    z_a, sib_a = halo(own_a), swap(own_a)
    both = (w2, g2, w3, g3)
    inner_b = spatial(spatial_kernel, 7, "spatial_b")(z_b, own_b, sib_b, *both)
    before_b = onward(inner_b)
    inner_a = spatial(spatial_kernel, 7, "spatial_a")(z_a, own_a, sib_a, *both)
    before_a = onward(inner_a)
    late, part = call(
        temporal_late_kernel,
        [pair_shape(), jax.ShapeDtypeStruct((C, PAIR), F32)],
        5,
        "temporal_late",
        moved=2000000,
    )(ts[1], inner_b, inner_a, before_b, inner_a)
    keep, send = call(temporal_last_kernel, [pair_shape()] * 2, 4, "temporal_last", moved=1500000)(
        ts[1], part, before_a, late
    )
    got = swap(send)
    out = unpack(unpack_got_kernel, got, unpack(unpack_keep_kernel, keep))
    return jnp.transpose(out, (0, 2, 1))[None]


def solution(mesh):
    placed = (P("frames", "rows", None, None), P(), P(), P())
    return jax.shard_map(
        on_device,
        mesh=mesh,
        in_specs=placed,
        out_specs=P("frames", "rows", None, None),
        check_vma=False,
    )
```

```python
import functools

import jax
import jax.numpy as jnp
from jax import lax
from jax.experimental import pallas as pl
from jax.experimental.pallas import tpu as pltpu
from jax.sharding import PartitionSpec as P

C = 192
W = 320
PAIR = 2 * W
LANES = 128
EPS = 1e-06
F32 = jnp.float32
BF16 = jnp.bfloat16
VMEM = pl.BlockSpec(memory_space=pltpu.VMEM)
ANY = pl.BlockSpec(memory_space=pl.ANY)
LIMIT = 20 << 20


def call(kernel, outs, n_in, name, scratch=(), flops=0, moved=0, in_specs=None, out_specs=None, aliases=None):
    many = isinstance(outs, (list, tuple))
    if out_specs is None:
        out_specs = [VMEM] * len(outs) if many else VMEM
    return pl.pallas_call(
        kernel,
        out_shape=outs,
        in_specs=in_specs or [VMEM] * n_in,
        out_specs=out_specs,
        scratch_shapes=list(scratch),
        input_output_aliases=aliases or {},
        compiler_params=pltpu.CompilerParams(vmem_limit_bytes=LIMIT),
        cost_estimate=pl.CostEstimate(flops=flops, bytes_accessed=moved, transcendentals=0),
        name=name,
    )


def pair_shape():
    return jax.ShapeDtypeStruct((C, PAIR), BF16)


def core_index():
    return lax.rem(lax.axis_index("frames"), 2)


def gain_column(g, k):
    return jnp.broadcast_to(g[k : k + 1, :] * 0.5, (LANES, C)).T


def transpose_taps(source, wt):
    for di in range(3):
        for dj in range(3):
            wt[dj * C : (dj + 1) * C, di * C : (di + 1) * C] = source[di, dj].T


def weights_kernel(sw, g, tw, w0, w1, w2, w3, g0, g1, g2, g3, t0, t1, held, taps, gains, sems, more_sems):
    gain_copy = pltpu.make_async_copy(g, gains, more_sems.at[0])
    tap_copy = pltpu.make_async_copy(tw, taps, more_sems.at[1])
    copies = [pltpu.make_async_copy(sw.at[k], held.at[k], sems.at[k]) for k in range(4)]
    gain_copy.start()
    for copy in copies:
        copy.start()
    tap_copy.start()
    gain_copy.wait()
    for k, gt in enumerate((g0, g1, g2, g3)):
        gt[...] = gain_column(gains, k)
    for k, wt in enumerate((w0, w1, w2, w3)):
        copies[k].wait()
        transpose_taps(held.at[k], wt)
    tap_copy.wait()
    for b, wt in enumerate((t0, t1)):
        for tap in range(3):
            wt[:, tap * C : (tap + 1) * C] = taps[b, tap].T


def in_hbm(x):
    return pltpu.with_memory_space_constraint(x, pltpu.HBM)


def prepare(weights, gains, taps):
    shape = jax.ShapeDtypeStruct
    outs = call(
        weights_kernel,
        [shape((3 * C, 3 * C), BF16)] * 4 + [shape((C, LANES), F32)] * 4 + [shape((C, 3 * C), BF16)] * 2,
        3,
        "weights",
        scratch=[
            pltpu.VMEM((4, 3, 3, C, C), BF16),
            pltpu.VMEM((2, 3, C, C), BF16),
            pltpu.VMEM((4, C), F32),
            pltpu.SemaphoreType.DMA((4,)),
            pltpu.SemaphoreType.DMA((2,)),
        ],
        moved=6000000,
        in_specs=[ANY] * 3,
    )(in_hbm(weights), in_hbm(gains), in_hbm(taps))
    return outs[:4], outs[4:8], outs[8:]


def pack_kernel(v, both, rows, sems):
    core = core_index()
    order = (2 - 2 * core, 3 - 2 * core, 2 * core, 2 * core + 1)
    copies = [pltpu.make_async_copy(v.at[order[i]], rows.at[i], sems.at[i]) for i in range(4)]
    for copy in copies:
        copy.start()
    for i in range(4):
        copies[i].wait()
        both[i // 2, :, (i % 2) * W : (i % 2 + 1) * W] = rows[i]


def pack_pair(rows, pair, dst):
    dst[:, :W] = rows[2 * pair]
    dst[:, W:] = rows[2 * pair + 1]


def join_kernel(mine, other, owned, sib):
    owned[0] = mine[1]
    pack_pair(other, core_index(), owned.at[1])
    pack_pair(other, 1 - core_index(), sib)


def unpack_rows(x, out, rows, sems, pair):
    copies = []
    for i in range(2):
        rows[i] = x[:, i * W : (i + 1) * W]
        copy = pltpu.make_async_copy(rows.at[i], out.at[2 * pair + i], sems.at[i])
        copy.start()
        copies.append(copy)
    for copy in copies:
        copy.wait()


def unpack_keep_kernel(keep, out, rows, sems):
    unpack_rows(keep, out, rows, sems, core_index())


def unpack_got_kernel(got, part, out, rows, sems):
    del part
    unpack_rows(got, out, rows, sems, 1 - core_index())


def unpack(kernel, x, *part):
    return call(
        kernel,
        jax.ShapeDtypeStruct((4, C, W), BF16),
        1 + len(part),
        "unpack",
        scratch=[pltpu.VMEM((2, C, W), BF16), pltpu.SemaphoreType.DMA((2,))],
        moved=500000,
        in_specs=[VMEM] + [ANY] * len(part),
        out_specs=ANY,
        aliases={1: 0} if part else None,
    )(x, *part)


def tiles_of(x):
    return [x[:, t * LANES : (t + 1) * LANES] for t in range(x.shape[1] // LANES)]


def activate(x, gain, valid):
    x = x.astype(F32)
    scale = lax.rsqrt(jnp.sum(x * x, axis=0, keepdims=True) * (1.0 / C) + EPS)
    if valid is not None:
        scale = scale * valid
    h = x * scale * gain
    return (h + h * jnp.tanh(h)).astype(BF16)


def between(x, y):
    low = lax.broadcasted_iota(jnp.int32, (1, LANES), 1) < LANES // 2
    turned = [pltpu.roll(t, LANES // 2, 1) for t in x[2:] + y[:3]]
    return [jnp.where(low, turned[i], turned[i + 1]) for i in range(5)]


def stack(rows, at, x, y):
    for t, (above, middle, below) in enumerate(zip(x, between(x, y), y)):
        lanes = slice(at + t * LANES, at + (t + 1) * LANES)
        rows[:C, lanes] = above
        rows[C : 2 * C, lanes] = middle
        rows[2 * C :, lanes] = below


def convolved(weight, rows):
    lane = lax.broadcasted_iota(jnp.int32, (1, LANES), 1)
    out = []
    for at in range(0, rows.shape[1], PAIR):
        product = jnp.dot(weight[...], rows[:, at : at + PAIR], preferred_element_type=F32)
        left, middle, right = (tiles_of(product[dj * C : (dj + 1) * C]) for dj in range(3))
        left = [pltpu.roll(t, 1, 1) for t in left]
        right = [pltpu.roll(t, LANES - 1, 1) for t in right]
        for t in range(5):
            a = jnp.where(lane == 0, left[t - 1] if t else 0.0, left[t])
            b = jnp.where(lane == LANES - 1, right[t + 1] if t < 4 else 0.0, right[t])
            if t == W // LANES:
                a = jnp.where(lane == W % LANES, 0.0, a)
                b = jnp.where(lane == W % LANES - 1, 0.0, b)
            out.append(middle[t] + a + b)
    return out


def either(first, x, y):
    return [jnp.where(first, s, t) for s, t in zip(x, y)]


def near_body(own, sib, w1, g1, g2, act1, act2, s1):
    is0 = core_index() == 0
    gain = g1[...]
    own = [activate(t, gain, None) for t in own]
    sib = [activate(t, gain, None) for t in sib]
    stack(s1, 0, either(is0, own, sib), either(is0, sib, own))
    gain = g2[...]
    for t, x in enumerate(convolved(w1, s1)):
        lanes = slice(t * LANES, (t + 1) * LANES)
        act1[:, lanes] = own[t]
        act2[:, lanes] = activate(x.astype(BF16), gain, None)


def near_mine_kernel(mine, *rest):
    near_body(tiles_of(mine.at[1]), tiles_of(mine.at[0]), *rest)


def near_other_kernel(owned, sib, *rest):
    near_body(tiles_of(owned.at[1]), tiles_of(sib), *rest)


def near(kernel, arrays, w1, g1, g2):
    return call(
        kernel,
        [pair_shape()] * 2,
        len(arrays) + 3,
        "near",
        scratch=[pltpu.VMEM((3 * C, PAIR), BF16)],
        flops=2 * C * C * 9 * PAIR,
        moved=2000000,
    )(*arrays, w1, g1, g2)


def far_body(z, own, act1, act2, w1, g1, w2, g2, out, s1, s2):
    core, row = core_index(), lax.axis_index("rows")
    is0 = core == 0
    top = is0 & (row == 0)
    bottom = (core == 1) & (row == lax.axis_size("rows") - 1)
    gain = g1[...]
    z = [activate(t, gain, None) for t in z]
    stack(s1, 0, either(is0, z, act1), either(is0, act1, z))
    lane = lax.broadcasted_iota(jnp.int32, (1, LANES), 1)
    gain = g2[...]
    far = []
    for t, x in enumerate(convolved(w1, s1)):
        pixel = lane + t * LANES
        outside = ((pixel < W) & top) | ((pixel >= W) & bottom)
        far.append(activate(x.astype(BF16), gain, jnp.where(outside, 0.0, 1.0).astype(F32)))
    stack(s2, 0, either(is0, far, act2), either(is0, act2, far))
    for t, (x, y) in enumerate(zip(own, convolved(w2, s2))):
        out[:, t * LANES : (t + 1) * LANES] = (x.astype(F32) + y).astype(BF16)


def far_pick_kernel(pick, z, owned, act1_m, act2_m, act1_o, act2_o, *rest):
    is_mine = core_index() == pick

    def chosen(x, y):
        return either(is_mine, tiles_of(x), tiles_of(y))

    far_body(
        chosen(z.at[1], z.at[0]),
        chosen(owned.at[0], owned.at[1]),
        chosen(act1_m, act1_o),
        chosen(act2_m, act2_o),
        *rest,
    )


def far(kernel, arrays, w1, g1, w2, g2):
    return call(
        kernel,
        pair_shape(),
        len(arrays) + 4,
        "far",
        scratch=[pltpu.VMEM((3 * C, PAIR), BF16)] * 2,
        flops=2 * C * C * 9 * 2 * PAIR,
        moved=4000000,
    )(*arrays, w1, g1, w2, g2)


def spatial_body(z, own, sib, w1, g1, w2, g2, out, s1, s2):
    core, row = core_index(), lax.axis_index("rows")
    is0 = core == 0
    top = is0 & (row == 0)
    bottom = (core == 1) & (row == lax.axis_size("rows") - 1)
    gain = g1[...]
    above, mid, below = [], [], []
    for tz, to, ts in zip(z, own, sib):
        above.append(activate(jnp.where(is0, tz, ts), gain, None))
        mid.append(activate(to, gain, None))
        below.append(activate(jnp.where(is0, ts, tz), gain, None))
    stack(s1, 0, above, mid)
    stack(s1, PAIR, mid, below)
    lane = lax.broadcasted_iota(jnp.int32, (1, LANES), 1)
    gain = g2[...]
    act = []
    for t, x in enumerate(convolved(w1, s1)):
        pixel = lane + t * LANES
        outside = ((pixel < W) & top) | ((pixel >= 3 * W) & bottom)
        act.append(activate(x.astype(BF16), gain, jnp.where(outside, 0.0, 1.0).astype(F32)))
    stack(s2, 0, act[:5], act[5:])
    for t, (x, y) in enumerate(zip(own, convolved(w2, s2))):
        out[:, t * LANES : (t + 1) * LANES] = (x.astype(F32) + y).astype(BF16)


def spatial_kernel(z, own, sib, *rest):
    spatial_body(tiles_of(z), tiles_of(own), tiles_of(sib), *rest)


def spatial(kernel, n_in, name):
    return call(
        kernel,
        pair_shape(),
        n_in,
        name,
        scratch=[pltpu.VMEM((3 * C, 2 * PAIR), BF16), pltpu.VMEM((3 * C, PAIR), BF16)],
        flops=2 * C * C * 9 * 3 * PAIR,
        moved=4000000,
    )


def mixed(wt, x0, x1, x2):
    total = x0[...].astype(F32)
    for tap, x in enumerate((x0, x1, x2)):
        total = total + jnp.dot(
            wt[:, tap * C : (tap + 1) * C], x[...], preferred_element_type=F32
        )
    return total.astype(BF16)


def temporal_kernel(wt, x0, x1, x2, out):
    out[...] = mixed(wt, x0, x1, x2)


def temporal(wt, x0, x1, x2):
    return call(
        temporal_kernel, pair_shape(), 4, "temporal", flops=2 * C * C * 3 * PAIR, moved=1300000
    )(wt, x0, x1, x2)


def temporal_late_kernel(wt, x0, x1, x2, y0, out, part):
    out[...] = mixed(wt, x0, x1, x2)
    total = y0[...].astype(F32)
    for tap, y in enumerate((y0, x2)):
        total = total + jnp.dot(
            wt[:, tap * C : (tap + 1) * C], y[...], preferred_element_type=F32
        )
    part[...] = total


def temporal_last_kernel(wt, part, y2, late, keep, send):
    early = part[...] + jnp.dot(wt[:, 2 * C :], y2[...], preferred_element_type=F32)
    early = early.astype(BF16)
    is0 = core_index() == 0
    other = late[...]
    keep[...] = jnp.where(is0, early, other)
    send[...] = jnp.where(is0, other, early)


def on_device(video, spatial_weights, norm_gains, temporal_weights):
    frames, rows = lax.axis_size("frames"), lax.axis_size("rows")
    swaps = [(i, i ^ 1) for i in range(frames)]
    across = []
    for f in range(frames):
        for r in range(rows):
            to = r + 1 if f % 2 else r - 1
            if 0 <= to < rows:
                across.append((f * rows + r, (f ^ 1) * rows + to))
    later = [(i, i + 2) for i in range(frames - 2)]

    def swap(x):
        return lax.ppermute(x, "frames", swaps)

    def halo(x):
        return lax.ppermute(x, ("frames", "rows"), across)

    def onward(x):
        return lax.ppermute(x, "frames", later)

    raw = jnp.transpose(video[0], (0, 2, 1))
    view = in_hbm(raw)
    mine = call(
        pack_kernel,
        jax.ShapeDtypeStruct((2, C, PAIR), BF16),
        1,
        "pack",
        scratch=[pltpu.VMEM((4, C, W), BF16), pltpu.SemaphoreType.DMA((4,))],
        moved=1000000,
        in_specs=[ANY],
    )(view)
    arrived = pltpu.with_memory_space_constraint(swap(raw), pltpu.VMEM)
    owned, sib_o = call(join_kernel, [jax.ShapeDtypeStruct((2, C, PAIR), BF16), pair_shape()], 2, "join", moved=1000)(
        mine, arrived
    )
    z = halo(owned)
    (w0, w1, w2, w3), (g0, g1, g2, g3), ts = prepare(spatial_weights, norm_gains, temporal_weights)

    near_m = near(near_mine_kernel, (mine,), w0, g0, g1)
    near_o = near(near_other_kernel, (owned, sib_o), w0, g0, g1)
    arrays = (z, owned, *near_m, *near_o)
    inner_b = far(functools.partial(far_pick_kernel, 1), arrays, w0, g0, w1, g1)
    before_b = onward(inner_b)
    inner_a = far(functools.partial(far_pick_kernel, 0), arrays, w0, g0, w1, g1)
    before_a = onward(inner_a)

    own_b = temporal(ts[0], inner_b, inner_a, before_b)
    z_b, sib_b = halo(own_b), swap(own_b)
    own_a = temporal(ts[0], inner_a, before_b, before_a)
    z_a, sib_a = halo(own_a), swap(own_a)
    both = (w2, g2, w3, g3)
    inner_b = spatial(spatial_kernel, 7, "spatial_b")(z_b, own_b, sib_b, *both)
    before_b = onward(inner_b)
    inner_a = spatial(spatial_kernel, 7, "spatial_a")(z_a, own_a, sib_a, *both)
    before_a = onward(inner_a)
    late, part = call(
        temporal_late_kernel,
        [pair_shape(), jax.ShapeDtypeStruct((C, PAIR), F32)],
        5,
        "temporal_late",
        moved=2000000,
    )(ts[1], inner_b, inner_a, before_b, inner_a)
    keep, send = call(temporal_last_kernel, [pair_shape()] * 2, 4, "temporal_last", moved=1500000)(
        ts[1], part, before_a, late
    )
    got = swap(send)
    out = unpack(unpack_got_kernel, got, unpack(unpack_keep_kernel, keep))
    return jnp.transpose(out, (0, 2, 1))[None]


def solution(mesh):
    placed = (P("frames", "rows", None, None), P(), P(), P())
    return jax.shard_map(
        on_device,
        mesh=mesh,
        in_specs=placed,
        out_specs=P("frames", "rows", None, None),
        check_vma=False,
    )
```

```python
import functools

import jax
import jax.numpy as jnp
from jax import lax
from jax.experimental import pallas as pl
from jax.experimental.pallas import tpu as pltpu
from jax.sharding import PartitionSpec as P

C = 192
W = 320
PAIR = 2 * W
LANES = 128
EPS = 1e-06
F32 = jnp.float32
BF16 = jnp.bfloat16
VMEM = pl.BlockSpec(memory_space=pltpu.VMEM)
ANY = pl.BlockSpec(memory_space=pl.ANY)
LIMIT = 20 << 20


def call(kernel, outs, n_in, name, scratch=(), flops=0, moved=0, in_specs=None, out_specs=None, aliases=None):
    many = isinstance(outs, (list, tuple))
    if out_specs is None:
        out_specs = [VMEM] * len(outs) if many else VMEM
    return pl.pallas_call(
        kernel,
        out_shape=outs,
        in_specs=in_specs or [VMEM] * n_in,
        out_specs=out_specs,
        scratch_shapes=list(scratch),
        input_output_aliases=aliases or {},
        compiler_params=pltpu.CompilerParams(vmem_limit_bytes=LIMIT),
        cost_estimate=pl.CostEstimate(flops=flops, bytes_accessed=moved, transcendentals=0),
        name=name,
    )


def pair_shape():
    return jax.ShapeDtypeStruct((C, PAIR), BF16)


def core_index():
    return lax.rem(lax.axis_index("frames"), 2)


def gain_column(g, k):
    return jnp.broadcast_to(g[k : k + 1, :] * 0.5, (LANES, C)).T


def transpose_taps(source, wt, order):
    for place, di in enumerate(order):
        for dj in range(3):
            wt[dj * C : (dj + 1) * C, place * C : (place + 1) * C] = source[di, dj].T


def weights_kernel(sw, g, tw, w0, w1, w2, w3, far0, far1, g0, g1, g2, g3, t0, t1, held, taps, gains, sems, more_sems):
    gain_copy = pltpu.make_async_copy(g, gains, more_sems.at[0])
    tap_copy = pltpu.make_async_copy(tw, taps, more_sems.at[1])
    copies = [pltpu.make_async_copy(sw.at[k], held.at[k], sems.at[k]) for k in range(4)]
    gain_copy.start()
    for copy in copies:
        copy.start()
    tap_copy.start()
    gain_copy.wait()
    for k, gt in enumerate((g0, g1, g2, g3)):
        gt[...] = gain_column(gains, k)
    core = core_index()
    by_core = (2 * core, 1, 2 - 2 * core)
    for k, wt in enumerate((w0, w1, w2, w3)):
        copies[k].wait()
        transpose_taps(held.at[k], wt, range(3))
        if k < 2:
            transpose_taps(held.at[k], (far0, far1)[k], by_core)
    tap_copy.wait()
    for b, wt in enumerate((t0, t1)):
        for tap in range(3):
            wt[:, tap * C : (tap + 1) * C] = taps[b, tap].T


def in_hbm(x):
    return pltpu.with_memory_space_constraint(x, pltpu.HBM)


def prepare(weights, gains, taps):
    shape = jax.ShapeDtypeStruct
    outs = call(
        weights_kernel,
        [shape((3 * C, 3 * C), BF16)] * 6 + [shape((C, LANES), F32)] * 4 + [shape((C, 3 * C), BF16)] * 2,
        3,
        "weights",
        scratch=[
            pltpu.VMEM((4, 3, 3, C, C), BF16),
            pltpu.VMEM((2, 3, C, C), BF16),
            pltpu.VMEM((4, C), F32),
            pltpu.SemaphoreType.DMA((4,)),
            pltpu.SemaphoreType.DMA((2,)),
        ],
        moved=6000000,
        in_specs=[ANY] * 3,
    )(in_hbm(weights), in_hbm(gains), in_hbm(taps))
    return outs[:6], outs[6:10], outs[10:]


def pack_kernel(v, both, rows, sems):
    core = core_index()
    order = (2 - 2 * core, 3 - 2 * core, 2 * core, 2 * core + 1)
    copies = [pltpu.make_async_copy(v.at[order[i]], rows.at[i], sems.at[i]) for i in range(4)]
    for copy in copies:
        copy.start()
    for i in range(4):
        copies[i].wait()
        both[i // 2, :, (i % 2) * W : (i % 2 + 1) * W] = rows[i]


def pack_pair(rows, pair, dst):
    dst[:, :W] = rows[2 * pair]
    dst[:, W:] = rows[2 * pair + 1]


def join_kernel(mine, other, owned, sib):
    owned[0] = mine[1]
    pack_pair(other, core_index(), owned.at[1])
    pack_pair(other, 1 - core_index(), sib)


def unpack_rows(x, out, rows, sems, pair):
    copies = []
    for i in range(2):
        rows[i] = x[:, i * W : (i + 1) * W]
        copy = pltpu.make_async_copy(rows.at[i], out.at[2 * pair + i], sems.at[i])
        copy.start()
        copies.append(copy)
    for copy in copies:
        copy.wait()


def unpack_keep_kernel(keep, out, rows, sems):
    unpack_rows(keep, out, rows, sems, core_index())


def unpack_got_kernel(got, part, out, rows, sems):
    del part
    unpack_rows(got, out, rows, sems, 1 - core_index())


def unpack(kernel, x, *part):
    return call(
        kernel,
        jax.ShapeDtypeStruct((4, C, W), BF16),
        1 + len(part),
        "unpack",
        scratch=[pltpu.VMEM((2, C, W), BF16), pltpu.SemaphoreType.DMA((2,))],
        moved=500000,
        in_specs=[VMEM] + [ANY] * len(part),
        out_specs=ANY,
        aliases={1: 0} if part else None,
    )(x, *part)


def tiles_of(x):
    return [x[:, t * LANES : (t + 1) * LANES] for t in range(x.shape[1] // LANES)]


def activate(x, gain, valid):
    x = x.astype(F32)
    scale = lax.rsqrt(jnp.sum(x * x, axis=0, keepdims=True) * (1.0 / C) + EPS)
    if valid is not None:
        scale = scale * valid
    h = x * scale * gain
    return (h + h * jnp.tanh(h)).astype(BF16)


def between(x, y):
    low = lax.broadcasted_iota(jnp.int32, (1, LANES), 1) < LANES // 2
    turned = [pltpu.roll(t, LANES // 2, 1) for t in x[2:] + y[:3]]
    return [jnp.where(low, turned[i], turned[i + 1]) for i in range(5)]


def stack(rows, at, x, y):
    for t, (above, middle, below) in enumerate(zip(x, between(x, y), y)):
        lanes = slice(at + t * LANES, at + (t + 1) * LANES)
        rows[:C, lanes] = above
        rows[C : 2 * C, lanes] = middle
        rows[2 * C :, lanes] = below


def put(rows, tiles, place, at=0):
    for t, x in enumerate(tiles):
        lanes = slice(at + t * LANES, at + (t + 1) * LANES)
        rows[place * C : (place + 1) * C, lanes] = x


def either(first, x, y):
    return [jnp.where(first, s, t) for s, t in zip(x, y)]


def middle(is0, far, near):
    return between(either(is0, far, near), either(is0, near, far))


def convolved(weight, rows):
    lane = lax.broadcasted_iota(jnp.int32, (1, LANES), 1)
    out = []
    for at in range(0, rows.shape[1], PAIR):
        product = jnp.dot(weight[...], rows[:, at : at + PAIR], preferred_element_type=F32)
        left, mid, right = (tiles_of(product[dj * C : (dj + 1) * C]) for dj in range(3))
        left = [pltpu.roll(t, 1, 1) for t in left]
        right = [pltpu.roll(t, LANES - 1, 1) for t in right]
        for t in range(5):
            a = jnp.where(lane == 0, left[t - 1] if t else 0.0, left[t])
            b = jnp.where(lane == LANES - 1, right[t + 1] if t < 4 else 0.0, right[t])
            if t == W // LANES:
                a = jnp.where(lane == W % LANES, 0.0, a)
                b = jnp.where(lane == W % LANES - 1, 0.0, b)
            out.append(mid[t] + a + b)
    return out


def inside(t):
    core, row = core_index(), lax.axis_index("rows")
    top = (core == 0) & (row == 0)
    bottom = (core == 1) & (row == lax.axis_size("rows") - 1)
    pixel = lax.broadcasted_iota(jnp.int32, (1, LANES), 1) + t * LANES
    outside = ((pixel < W) & top) | ((pixel >= W) & bottom)
    return jnp.where(outside, 0.0, 1.0).astype(F32)


def near_pick_kernel(pick, mine, owned, sib_o, w1, g1, w2, g2, part1, part2, s1, s2):
    is0 = core_index() == 0
    is_mine = core_index() == pick
    own = either(is_mine, tiles_of(mine.at[1]), tiles_of(owned.at[1]))
    sib = either(is_mine, tiles_of(mine.at[0]), tiles_of(sib_o))
    act = [activate(t, g1[...], None) for t in own]
    other = [activate(t, g1[...], None) for t in sib]
    none = [jnp.zeros_like(t) for t in act]
    put(s1, act, 0)
    put(s1, middle(is0, act, other), 1)
    put(s1, other, 2)
    inner = [activate(x.astype(BF16), g2[...], None) for x in convolved(w1, s1)]
    put(s2, middle(is0, none, act), 0)
    put(s2, act, 1)
    for t, x in enumerate(convolved(w1.at[:, C:], s2)):
        part1[:, t * LANES : (t + 1) * LANES] = x
    put(s2, middle(is0, none, inner), 0)
    put(s2, inner, 1)
    for t, (x, y) in enumerate(zip(own, convolved(w2.at[:, C:], s2))):
        part2[:, t * LANES : (t + 1) * LANES] = x.astype(F32) + y


def near(pick, mine, owned, sib_o, *weights):
    return call(
        functools.partial(near_pick_kernel, pick),
        [jax.ShapeDtypeStruct((C, PAIR), F32)] * 2,
        7,
        "near",
        scratch=[pltpu.VMEM((3 * C, PAIR), BF16), pltpu.VMEM((2 * C, PAIR), BF16)],
        flops=2 * C * C * 9 * PAIR,
        moved=2000000,
    )(mine, owned, sib_o, *weights)


def far_pick_kernel(pick, z, part1, part2, w1, g1, w2, g2, out, s2):
    is0 = core_index() == 0
    is_mine = core_index() == pick
    far = either(is_mine, tiles_of(z.at[1]), tiles_of(z.at[0]))
    far = [activate(t, g1[...], None) for t in far]
    none = [jnp.zeros_like(t) for t in far]
    put(s2, far, 0)
    put(s2, middle(is0, far, none), 1)
    inner = []
    for t, (x, y) in enumerate(zip(tiles_of(part1), convolved(w1.at[:, : 2 * C], s2))):
        inner.append(activate((x + y).astype(BF16), g2[...], inside(t)))
    put(s2, inner, 0)
    put(s2, middle(is0, inner, none), 1)
    for t, (x, y) in enumerate(zip(tiles_of(part2), convolved(w2.at[:, : 2 * C], s2))):
        out[:, t * LANES : (t + 1) * LANES] = (x + y).astype(BF16)


def far(pick, z, part1, part2, *weights):
    return call(
        functools.partial(far_pick_kernel, pick),
        pair_shape(),
        7,
        "far",
        scratch=[pltpu.VMEM((2 * C, PAIR), BF16)],
        flops=2 * C * C * 9 * 2 * PAIR,
        moved=4000000,
    )(z, part1, part2, *weights)


def spatial_body(z, own, sib, w1, g1, w2, g2, out, s1, s2):
    core, row = core_index(), lax.axis_index("rows")
    is0 = core == 0
    top = is0 & (row == 0)
    bottom = (core == 1) & (row == lax.axis_size("rows") - 1)
    gain = g1[...]
    above = [activate(t, gain, None) for t in either(is0, z, sib)]
    mid = [activate(t, gain, None) for t in own]
    below = [activate(t, gain, None) for t in either(is0, sib, z)]
    stack(s1, 0, above, mid)
    stack(s1, PAIR, mid, below)
    lane = lax.broadcasted_iota(jnp.int32, (1, LANES), 1)
    gain = g2[...]
    act = []
    for t, x in enumerate(convolved(w1, s1)):
        pixel = lane + t * LANES
        outside = ((pixel < W) & top) | ((pixel >= 3 * W) & bottom)
        act.append(activate(x.astype(BF16), gain, jnp.where(outside, 0.0, 1.0).astype(F32)))
    stack(s2, 0, act[:5], act[5:])
    for t, (x, y) in enumerate(zip(own, convolved(w2, s2))):
        out[:, t * LANES : (t + 1) * LANES] = (x.astype(F32) + y).astype(BF16)


def spatial_kernel(z, own, sib, *rest):
    spatial_body(tiles_of(z), tiles_of(own), tiles_of(sib), *rest)


def spatial_pick_kernel(pick, z, mine, owned, sib_o, *rest):
    is_mine = core_index() == pick

    def chosen(x, y):
        return either(is_mine, tiles_of(x), tiles_of(y))

    spatial_body(
        chosen(z.at[1], z.at[0]), chosen(mine.at[1], owned.at[1]), chosen(mine.at[0], sib_o), *rest
    )


def spatial(kernel, n_in, name):
    return call(
        kernel,
        pair_shape(),
        n_in,
        name,
        scratch=[pltpu.VMEM((3 * C, 2 * PAIR), BF16), pltpu.VMEM((3 * C, PAIR), BF16)],
        flops=2 * C * C * 9 * 3 * PAIR,
        moved=4000000,
    )


def mixed(wt, x0, x1, x2):
    total = x0[...].astype(F32)
    for tap, x in enumerate((x0, x1, x2)):
        total = total + jnp.dot(
            wt[:, tap * C : (tap + 1) * C], x[...], preferred_element_type=F32
        )
    return total.astype(BF16)


def temporal_kernel(wt, x0, x1, x2, out):
    out[...] = mixed(wt, x0, x1, x2)


def temporal(wt, x0, x1, x2):
    return call(
        temporal_kernel, pair_shape(), 4, "temporal", flops=2 * C * C * 3 * PAIR, moved=1300000
    )(wt, x0, x1, x2)


def temporal_late_kernel(wt, x0, x1, x2, y0, out, part):
    out[...] = mixed(wt, x0, x1, x2)
    total = y0[...].astype(F32)
    for tap, y in enumerate((y0, x2)):
        total = total + jnp.dot(
            wt[:, tap * C : (tap + 1) * C], y[...], preferred_element_type=F32
        )
    part[...] = total


def temporal_last_kernel(wt, part, y2, late, keep, send):
    early = part[...] + jnp.dot(wt[:, 2 * C :], y2[...], preferred_element_type=F32)
    early = early.astype(BF16)
    is0 = core_index() == 0
    other = late[...]
    keep[...] = jnp.where(is0, early, other)
    send[...] = jnp.where(is0, other, early)


def on_device(video, spatial_weights, norm_gains, temporal_weights):
    frames, rows = lax.axis_size("frames"), lax.axis_size("rows")
    swaps = [(i, i ^ 1) for i in range(frames)]
    across = []
    for f in range(frames):
        for r in range(rows):
            to = r + 1 if f % 2 else r - 1
            if 0 <= to < rows:
                across.append((f * rows + r, (f ^ 1) * rows + to))
    later = [(i, i + 2) for i in range(frames - 2)]

    def swap(x):
        return lax.ppermute(x, "frames", swaps)

    def halo(x):
        return lax.ppermute(x, ("frames", "rows"), across)

    def onward(x):
        return lax.ppermute(x, "frames", later)

    raw = jnp.transpose(video[0], (0, 2, 1))
    view = in_hbm(raw)
    mine = call(
        pack_kernel,
        jax.ShapeDtypeStruct((2, C, PAIR), BF16),
        1,
        "pack",
        scratch=[pltpu.VMEM((4, C, W), BF16), pltpu.SemaphoreType.DMA((4,))],
        moved=1000000,
        in_specs=[ANY],
    )(view)
    arrived = pltpu.with_memory_space_constraint(swap(raw), pltpu.VMEM)
    owned, sib_o = call(join_kernel, [jax.ShapeDtypeStruct((2, C, PAIR), BF16), pair_shape()], 2, "join", moved=1000)(
        mine, arrived
    )
    z = halo(owned)
    (w0, w1, w2, w3, far0, far1), (g0, g1, g2, g3), ts = prepare(spatial_weights, norm_gains, temporal_weights)

    block = (w0, g0, w1, g1)
    by_core = (far0, g0, far1, g1)
    parts = near(1, mine, owned, sib_o, *by_core)
    inner_b = far(1, z, *parts, *by_core)
    before_b = onward(inner_b)
    inner_a = spatial(functools.partial(spatial_pick_kernel, 0), 8, "spatial_a1")(z, mine, owned, sib_o, *block)
    before_a = onward(inner_a)

    own_b = temporal(ts[0], inner_b, inner_a, before_b)
    z_b, sib_b = halo(own_b), swap(own_b)
    own_a = temporal(ts[0], inner_a, before_b, before_a)
    z_a, sib_a = halo(own_a), swap(own_a)
    both = (w2, g2, w3, g3)
    inner_b = spatial(spatial_kernel, 7, "spatial_b")(z_b, own_b, sib_b, *both)
    before_b = onward(inner_b)
    inner_a = spatial(spatial_kernel, 7, "spatial_a")(z_a, own_a, sib_a, *both)
    before_a = onward(inner_a)
    late, part = call(
        temporal_late_kernel,
        [pair_shape(), jax.ShapeDtypeStruct((C, PAIR), F32)],
        5,
        "temporal_late",
        moved=2000000,
    )(ts[1], inner_b, inner_a, before_b, inner_a)
    keep, send = call(temporal_last_kernel, [pair_shape()] * 2, 4, "temporal_last", moved=1500000)(
        ts[1], part, before_a, late
    )
    got = swap(send)
    out = unpack(unpack_got_kernel, got, unpack(unpack_keep_kernel, keep))
    return jnp.transpose(out, (0, 2, 1))[None]


def solution(mesh):
    placed = (P("frames", "rows", None, None), P(), P(), P())
    return jax.shard_map(
        on_device,
        mesh=mesh,
        in_specs=placed,
        out_specs=P("frames", "rows", None, None),
        check_vma=False,
    )
```

```python
import functools

import jax
import jax.numpy as jnp
from jax import lax
from jax.experimental import pallas as pl
from jax.experimental.pallas import tpu as pltpu
from jax.sharding import PartitionSpec as P

C = 192
W = 320
PAIR = 2 * W
LANES = 128
EPS = 1e-06
F32 = jnp.float32
BF16 = jnp.bfloat16
VMEM = pl.BlockSpec(memory_space=pltpu.VMEM)
ANY = pl.BlockSpec(memory_space=pl.ANY)
LIMIT = 20 << 20


def call(kernel, outs, n_in, name, scratch=(), flops=0, moved=0, in_specs=None, out_specs=None, aliases=None):
    many = isinstance(outs, (list, tuple))
    if out_specs is None:
        out_specs = [VMEM] * len(outs) if many else VMEM
    return pl.pallas_call(
        kernel,
        out_shape=outs,
        in_specs=in_specs or [VMEM] * n_in,
        out_specs=out_specs,
        scratch_shapes=list(scratch),
        input_output_aliases=aliases or {},
        compiler_params=pltpu.CompilerParams(vmem_limit_bytes=LIMIT),
        cost_estimate=pl.CostEstimate(flops=flops, bytes_accessed=moved, transcendentals=0),
        name=name,
    )


def pair_shape():
    return jax.ShapeDtypeStruct((C, PAIR), BF16)


def core_index():
    return lax.rem(lax.axis_index("frames"), 2)


def gain_column(g, k):
    return jnp.broadcast_to(g[k : k + 1, :] * 0.5, (LANES, C)).T


def transpose_taps(source, wt, order):
    for place, di in enumerate(order):
        for dj in range(3):
            wt[dj * C : (dj + 1) * C, place * C : (place + 1) * C] = source[di, dj].T


def weights_kernel(sw, g, tw, w0, w1, w2, w3, far0, far1, g0, g1, g2, g3, t0, t1, held, taps, gains, sems, more_sems):
    gain_copy = pltpu.make_async_copy(g, gains, more_sems.at[0])
    tap_copy = pltpu.make_async_copy(tw, taps, more_sems.at[1])
    copies = [pltpu.make_async_copy(sw.at[k], held.at[k], sems.at[k]) for k in range(4)]
    gain_copy.start()
    for copy in copies:
        copy.start()
    tap_copy.start()
    gain_copy.wait()
    for k, gt in enumerate((g0, g1, g2, g3)):
        gt[...] = gain_column(gains, k)
    core = core_index()
    by_core = (2 * core, 1, 2 - 2 * core)
    for k, wt in enumerate((w0, w1, w2, w3)):
        copies[k].wait()
        transpose_taps(held.at[k], wt, range(3))
        if k < 2:
            transpose_taps(held.at[k], (far0, far1)[k], by_core)
    tap_copy.wait()
    for b, wt in enumerate((t0, t1)):
        for tap in range(3):
            wt[:, tap * C : (tap + 1) * C] = taps[b, tap].T


def in_hbm(x):
    return pltpu.with_memory_space_constraint(x, pltpu.HBM)


def prepare(weights, gains, taps):
    shape = jax.ShapeDtypeStruct
    outs = call(
        weights_kernel,
        [shape((3 * C, 3 * C), BF16)] * 6 + [shape((C, LANES), F32)] * 4 + [shape((C, 3 * C), BF16)] * 2,
        3,
        "weights",
        scratch=[
            pltpu.VMEM((4, 3, 3, C, C), BF16),
            pltpu.VMEM((2, 3, C, C), BF16),
            pltpu.VMEM((4, C), F32),
            pltpu.SemaphoreType.DMA((4,)),
            pltpu.SemaphoreType.DMA((2,)),
        ],
        moved=6000000,
        in_specs=[ANY] * 3,
    )(in_hbm(weights), in_hbm(gains), in_hbm(taps))
    return outs[:6], outs[6:10], outs[10:]


def pack_kernel(v, both, rows, sems):
    core = core_index()
    order = (2 - 2 * core, 3 - 2 * core, 2 * core, 2 * core + 1)
    copies = [pltpu.make_async_copy(v.at[order[i]], rows.at[i], sems.at[i]) for i in range(4)]
    for copy in copies:
        copy.start()
    for i in range(4):
        copies[i].wait()
        both[i // 2, :, (i % 2) * W : (i % 2 + 1) * W] = rows[i]


def pack_pair(rows, pair, dst):
    dst[:, :W] = rows[2 * pair]
    dst[:, W:] = rows[2 * pair + 1]


def join_kernel(mine, other, owned, sib):
    owned[0] = mine[1]
    pack_pair(other, core_index(), owned.at[1])
    pack_pair(other, 1 - core_index(), sib)


def unpack_rows(x, out, rows, sems, pair):
    copies = []
    for i in range(2):
        rows[i] = x[:, i * W : (i + 1) * W]
        copy = pltpu.make_async_copy(rows.at[i], out.at[2 * pair + i], sems.at[i])
        copy.start()
        copies.append(copy)
    for copy in copies:
        copy.wait()


def store_later_kernel(mine, other, out, rows, sems):
    @pl.when(core_index() == 1)
    def _():
        unpack_rows(mine, out, rows, sems, 1)
        unpack_rows(other, out, rows, sems, 0)


def store_earlier_kernel(pair, x, part, out, rows, sems):
    del part

    @pl.when(core_index() == 0)
    def _():
        unpack_rows(x, out, rows, sems, pair)


def store(kernel, arrays, *part):
    return call(
        kernel,
        jax.ShapeDtypeStruct((4, C, W), BF16),
        len(arrays) + len(part),
        "store",
        scratch=[pltpu.VMEM((2, C, W), BF16), pltpu.SemaphoreType.DMA((2,))],
        moved=500000,
        in_specs=[VMEM] * len(arrays) + [ANY] * len(part),
        out_specs=ANY,
        aliases={len(arrays): 0} if part else None,
    )(*arrays, *part)


def tiles_of(x):
    return [x[:, t * LANES : (t + 1) * LANES] for t in range(x.shape[1] // LANES)]


def activate(x, gain, valid):
    x = x.astype(F32)
    scale = lax.rsqrt(jnp.sum(x * x, axis=0, keepdims=True) * (1.0 / C) + EPS)
    if valid is not None:
        scale = scale * valid
    h = x * scale * gain
    return (h + h * jnp.tanh(h)).astype(BF16)


def between(x, y):
    low = lax.broadcasted_iota(jnp.int32, (1, LANES), 1) < LANES // 2
    turned = [pltpu.roll(t, LANES // 2, 1) for t in x[2:] + y[:3]]
    return [jnp.where(low, turned[i], turned[i + 1]) for i in range(5)]


def stack(rows, at, x, y):
    for t, (above, middle, below) in enumerate(zip(x, between(x, y), y)):
        lanes = slice(at + t * LANES, at + (t + 1) * LANES)
        rows[:C, lanes] = above
        rows[C : 2 * C, lanes] = middle
        rows[2 * C :, lanes] = below


def put(rows, tiles, place, at=0):
    for t, x in enumerate(tiles):
        lanes = slice(at + t * LANES, at + (t + 1) * LANES)
        rows[place * C : (place + 1) * C, lanes] = x


def either(first, x, y):
    return [jnp.where(first, s, t) for s, t in zip(x, y)]


def middle(is0, far, near):
    return between(either(is0, far, near), either(is0, near, far))


def convolved(weight, rows):
    lane = lax.broadcasted_iota(jnp.int32, (1, LANES), 1)
    out = []
    for at in range(0, rows.shape[1], PAIR):
        product = jnp.dot(weight[...], rows[:, at : at + PAIR], preferred_element_type=F32)
        left, mid, right = (tiles_of(product[dj * C : (dj + 1) * C]) for dj in range(3))
        left = [pltpu.roll(t, 1, 1) for t in left]
        right = [pltpu.roll(t, LANES - 1, 1) for t in right]
        for t in range(5):
            a = jnp.where(lane == 0, left[t - 1] if t else 0.0, left[t])
            b = jnp.where(lane == LANES - 1, right[t + 1] if t < 4 else 0.0, right[t])
            if t == W // LANES:
                a = jnp.where(lane == W % LANES, 0.0, a)
                b = jnp.where(lane == W % LANES - 1, 0.0, b)
            out.append(mid[t] + a + b)
    return out


def inside(t):
    core, row = core_index(), lax.axis_index("rows")
    top = (core == 0) & (row == 0)
    bottom = (core == 1) & (row == lax.axis_size("rows") - 1)
    pixel = lax.broadcasted_iota(jnp.int32, (1, LANES), 1) + t * LANES
    outside = ((pixel < W) & top) | ((pixel >= W) & bottom)
    return jnp.where(outside, 0.0, 1.0).astype(F32)


def near_pick_kernel(pick, mine, owned, sib_o, w1, g1, w2, g2, part1, part2, s1, s2):
    is0 = core_index() == 0
    is_mine = core_index() == pick
    own = either(is_mine, tiles_of(mine.at[1]), tiles_of(owned.at[1]))
    sib = either(is_mine, tiles_of(mine.at[0]), tiles_of(sib_o))
    act = [activate(t, g1[...], None) for t in own]
    other = [activate(t, g1[...], None) for t in sib]
    none = [jnp.zeros_like(t) for t in act]
    put(s1, act, 0)
    put(s1, middle(is0, act, other), 1)
    put(s1, other, 2)
    inner = [activate(x.astype(BF16), g2[...], None) for x in convolved(w1, s1)]
    put(s2, middle(is0, none, act), 0)
    put(s2, act, 1)
    for t, x in enumerate(convolved(w1.at[:, C:], s2)):
        part1[:, t * LANES : (t + 1) * LANES] = x
    put(s2, middle(is0, none, inner), 0)
    put(s2, inner, 1)
    for t, (x, y) in enumerate(zip(own, convolved(w2.at[:, C:], s2))):
        part2[:, t * LANES : (t + 1) * LANES] = x.astype(F32) + y


def near(pick, mine, owned, sib_o, *weights):
    return call(
        functools.partial(near_pick_kernel, pick),
        [jax.ShapeDtypeStruct((C, PAIR), F32)] * 2,
        7,
        "near",
        scratch=[pltpu.VMEM((3 * C, PAIR), BF16), pltpu.VMEM((2 * C, PAIR), BF16)],
        flops=2 * C * C * 9 * PAIR,
        moved=2000000,
    )(mine, owned, sib_o, *weights)


def far_pick_kernel(pick, z, part1, part2, w1, g1, w2, g2, out, s2):
    is0 = core_index() == 0
    is_mine = core_index() == pick
    far = either(is_mine, tiles_of(z.at[1]), tiles_of(z.at[0]))
    far = [activate(t, g1[...], None) for t in far]
    none = [jnp.zeros_like(t) for t in far]
    put(s2, far, 0)
    put(s2, middle(is0, far, none), 1)
    inner = []
    for t, (x, y) in enumerate(zip(tiles_of(part1), convolved(w1.at[:, : 2 * C], s2))):
        inner.append(activate((x + y).astype(BF16), g2[...], inside(t)))
    put(s2, inner, 0)
    put(s2, middle(is0, inner, none), 1)
    for t, (x, y) in enumerate(zip(tiles_of(part2), convolved(w2.at[:, : 2 * C], s2))):
        out[:, t * LANES : (t + 1) * LANES] = (x + y).astype(BF16)


def far(pick, z, part1, part2, *weights):
    return call(
        functools.partial(far_pick_kernel, pick),
        pair_shape(),
        7,
        "far",
        scratch=[pltpu.VMEM((2 * C, PAIR), BF16)],
        flops=2 * C * C * 9 * 2 * PAIR,
        moved=4000000,
    )(z, part1, part2, *weights)


def spatial_body(z, own, sib, w1, g1, w2, g2, out, s1, s2):
    core, row = core_index(), lax.axis_index("rows")
    is0 = core == 0
    top = is0 & (row == 0)
    bottom = (core == 1) & (row == lax.axis_size("rows") - 1)
    gain = g1[...]
    above = [activate(t, gain, None) for t in either(is0, z, sib)]
    mid = [activate(t, gain, None) for t in own]
    below = [activate(t, gain, None) for t in either(is0, sib, z)]
    stack(s1, 0, above, mid)
    stack(s1, PAIR, mid, below)
    lane = lax.broadcasted_iota(jnp.int32, (1, LANES), 1)
    gain = g2[...]
    act = []
    for t, x in enumerate(convolved(w1, s1)):
        pixel = lane + t * LANES
        outside = ((pixel < W) & top) | ((pixel >= 3 * W) & bottom)
        act.append(activate(x.astype(BF16), gain, jnp.where(outside, 0.0, 1.0).astype(F32)))
    stack(s2, 0, act[:5], act[5:])
    for t, (x, y) in enumerate(zip(own, convolved(w2, s2))):
        out[:, t * LANES : (t + 1) * LANES] = (x.astype(F32) + y).astype(BF16)


def spatial_kernel(z, own, sib, *rest):
    spatial_body(tiles_of(z), tiles_of(own), tiles_of(sib), *rest)


def spatial_pick_kernel(pick, z, mine, owned, sib_o, *rest):
    is_mine = core_index() == pick

    def chosen(x, y):
        return either(is_mine, tiles_of(x), tiles_of(y))

    spatial_body(
        chosen(z.at[1], z.at[0]), chosen(mine.at[1], owned.at[1]), chosen(mine.at[0], sib_o), *rest
    )


def spatial(kernel, n_in, name):
    return call(
        kernel,
        pair_shape(),
        n_in,
        name,
        scratch=[pltpu.VMEM((3 * C, 2 * PAIR), BF16), pltpu.VMEM((3 * C, PAIR), BF16)],
        flops=2 * C * C * 9 * 3 * PAIR,
        moved=4000000,
    )


def mixed(wt, x0, x1, x2):
    total = x0[...].astype(F32)
    for tap, x in enumerate((x0, x1, x2)):
        total = total + jnp.dot(
            wt[:, tap * C : (tap + 1) * C], x[...], preferred_element_type=F32
        )
    return total.astype(BF16)


def temporal_kernel(wt, x0, x1, x2, out):
    out[...] = mixed(wt, x0, x1, x2)


def temporal(wt, x0, x1, x2):
    return call(
        temporal_kernel, pair_shape(), 4, "temporal", flops=2 * C * C * 3 * PAIR, moved=1300000
    )(wt, x0, x1, x2)


def temporal_late_kernel(wt, x0, x1, x2, y0, out, part):
    out[...] = mixed(wt, x0, x1, x2)
    total = y0[...].astype(F32)
    for tap, y in enumerate((y0, x2)):
        total = total + jnp.dot(
            wt[:, tap * C : (tap + 1) * C], y[...], preferred_element_type=F32
        )
    part[...] = total


def temporal_last_kernel(wt, part, y2, out):
    last = jnp.dot(wt[:, 2 * C :], y2[...], preferred_element_type=F32)
    out[...] = (part[...] + last).astype(BF16)


def on_device(video, spatial_weights, norm_gains, temporal_weights):
    frames, rows = lax.axis_size("frames"), lax.axis_size("rows")
    swaps = [(i, i ^ 1) for i in range(frames)]
    across = []
    for f in range(frames):
        for r in range(rows):
            to = r + 1 if f % 2 else r - 1
            if 0 <= to < rows:
                across.append((f * rows + r, (f ^ 1) * rows + to))
    later = [(i, i + 2) for i in range(frames - 2)]

    def swap(x):
        return lax.ppermute(x, "frames", swaps)

    def halo(x):
        return lax.ppermute(x, ("frames", "rows"), across)

    def onward(x):
        return lax.ppermute(x, "frames", later)

    raw = jnp.transpose(video[0], (0, 2, 1))
    view = in_hbm(raw)
    mine = call(
        pack_kernel,
        jax.ShapeDtypeStruct((2, C, PAIR), BF16),
        1,
        "pack",
        scratch=[pltpu.VMEM((4, C, W), BF16), pltpu.SemaphoreType.DMA((4,))],
        moved=1000000,
        in_specs=[ANY],
    )(view)
    arrived = pltpu.with_memory_space_constraint(swap(raw), pltpu.VMEM)
    owned, sib_o = call(join_kernel, [jax.ShapeDtypeStruct((2, C, PAIR), BF16), pair_shape()], 2, "join", moved=1000)(
        mine, arrived
    )
    z = halo(owned)
    (w0, w1, w2, w3, far0, far1), (g0, g1, g2, g3), ts = prepare(spatial_weights, norm_gains, temporal_weights)

    block = (w0, g0, w1, g1)
    by_core = (far0, g0, far1, g1)
    parts = near(1, mine, owned, sib_o, *by_core)
    inner_b = far(1, z, *parts, *by_core)
    before_b = onward(inner_b)
    inner_a = spatial(functools.partial(spatial_pick_kernel, 0), 8, "spatial_a1")(z, mine, owned, sib_o, *block)
    before_a = onward(inner_a)

    own_b = temporal(ts[0], inner_b, inner_a, before_b)
    z_b, sib_b = halo(own_b), swap(own_b)
    own_a = temporal(ts[0], inner_a, before_b, before_a)
    z_a, sib_a = halo(own_a), swap(own_a)
    both = (w2, g2, w3, g3)
    inner_b = spatial(spatial_kernel, 7, "spatial_b")(z_b, own_b, sib_b, *both)
    before_b = onward(inner_b)
    inner_a = spatial(spatial_kernel, 7, "spatial_a")(z_a, own_a, sib_a, *both)
    before_a = onward(inner_a)
    late, part = call(
        temporal_late_kernel,
        [pair_shape(), jax.ShapeDtypeStruct((C, PAIR), F32)],
        5,
        "temporal_late",
        moved=2000000,
    )(ts[1], inner_b, inner_a, before_b, inner_a)
    late_other = swap(late)
    out = store(store_later_kernel, (late, late_other))
    early = call(temporal_last_kernel, pair_shape(), 3, "temporal_last", moved=1500000)(ts[1], part, before_a)
    early_other = swap(early)
    out = store(functools.partial(store_earlier_kernel, 0), (early,), out)
    out = store(functools.partial(store_earlier_kernel, 1), (early_other,), out)
    return jnp.transpose(out, (0, 2, 1))[None]


def solution(mesh):
    placed = (P("frames", "rows", None, None), P(), P(), P())
    return jax.shard_map(
        on_device,
        mesh=mesh,
        in_specs=placed,
        out_specs=P("frames", "rows", None, None),
        check_vma=False,
    )
```

```python
import functools

import jax
import jax.numpy as jnp
from jax import lax
from jax.experimental import pallas as pl
from jax.experimental.pallas import tpu as pltpu
from jax.sharding import PartitionSpec as P

C = 192
W = 320
PAIR = 2 * W
LANES = 128
EPS = 1e-06
F32 = jnp.float32
BF16 = jnp.bfloat16
VMEM = pl.BlockSpec(memory_space=pltpu.VMEM)
ANY = pl.BlockSpec(memory_space=pl.ANY)
LIMIT = 20 << 20


def call(kernel, outs, n_in, name, scratch=(), flops=0, moved=0, in_specs=None, out_specs=None, aliases=None):
    many = isinstance(outs, (list, tuple))
    if out_specs is None:
        out_specs = [VMEM] * len(outs) if many else VMEM
    return pl.pallas_call(
        kernel,
        out_shape=outs,
        in_specs=in_specs or [VMEM] * n_in,
        out_specs=out_specs,
        scratch_shapes=list(scratch),
        input_output_aliases=aliases or {},
        compiler_params=pltpu.CompilerParams(vmem_limit_bytes=LIMIT),
        cost_estimate=pl.CostEstimate(flops=flops, bytes_accessed=moved, transcendentals=0),
        name=name,
    )


def pair_shape():
    return jax.ShapeDtypeStruct((C, PAIR), BF16)


def core_index():
    return lax.rem(lax.axis_index("frames"), 2)


def gain_column(g, k):
    return jnp.broadcast_to(g[k : k + 1, :] * 0.5, (LANES, C)).T


def transpose_taps(source, wt, order):
    for place, di in enumerate(order):
        for dj in range(3):
            wt[dj * C : (dj + 1) * C, place * C : (place + 1) * C] = source[di, dj].T


def weights_kernel(sw, g, tw, w0, w1, w2, w3, far0, far1, g0, g1, g2, g3, t0, t1, held, taps, gains, sems, more_sems):
    gain_copy = pltpu.make_async_copy(g, gains, more_sems.at[0])
    tap_copy = pltpu.make_async_copy(tw, taps, more_sems.at[1])
    copies = [pltpu.make_async_copy(sw.at[k], held.at[k], sems.at[k]) for k in range(4)]
    gain_copy.start()
    for copy in copies:
        copy.start()
    tap_copy.start()
    gain_copy.wait()
    for k, gt in enumerate((g0, g1, g2, g3)):
        gt[...] = gain_column(gains, k)
    core = core_index()
    by_core = (2 * core, 1, 2 - 2 * core)
    for k, wt in enumerate((w0, w1, w2, w3)):
        copies[k].wait()
        transpose_taps(held.at[k], wt, range(3))
        if k < 2:
            transpose_taps(held.at[k], (far0, far1)[k], by_core)
    tap_copy.wait()
    for b, wt in enumerate((t0, t1)):
        for tap in range(3):
            wt[:, tap * C : (tap + 1) * C] = taps[b, tap].T


def in_hbm(x):
    return pltpu.with_memory_space_constraint(x, pltpu.HBM)


def prepare(weights, gains, taps):
    shape = jax.ShapeDtypeStruct
    outs = call(
        weights_kernel,
        [shape((3 * C, 3 * C), BF16)] * 6 + [shape((C, LANES), F32)] * 4 + [shape((C, 3 * C), BF16)] * 2,
        3,
        "weights",
        scratch=[
            pltpu.VMEM((4, 3, 3, C, C), BF16),
            pltpu.VMEM((2, 3, C, C), BF16),
            pltpu.VMEM((4, C), F32),
            pltpu.SemaphoreType.DMA((4,)),
            pltpu.SemaphoreType.DMA((2,)),
        ],
        moved=6000000,
        in_specs=[ANY] * 3,
    )(in_hbm(weights), in_hbm(gains), in_hbm(taps))
    return outs[:6], outs[6:10], outs[10:]


def pack_kernel(v, both, rows, sems):
    core = core_index()
    order = (2 - 2 * core, 3 - 2 * core, 2 * core, 2 * core + 1)
    copies = [pltpu.make_async_copy(v.at[order[i]], rows.at[i], sems.at[i]) for i in range(4)]
    for copy in copies:
        copy.start()
    for i in range(4):
        copies[i].wait()
        both[i // 2, :, (i % 2) * W : (i % 2 + 1) * W] = rows[i]


def pack_pair(rows, pair, dst):
    dst[:, :W] = rows[2 * pair]
    dst[:, W:] = rows[2 * pair + 1]


def join_kernel(mine, other, owned, sib):
    owned[0] = mine[1]
    pack_pair(other, core_index(), owned.at[1])
    pack_pair(other, 1 - core_index(), sib)


def unpack_rows(x, out, rows, sems, pair):
    copies = []
    for i in range(2):
        rows[i] = x[:, i * W : (i + 1) * W]
        copy = pltpu.make_async_copy(rows.at[i], out.at[2 * pair + i], sems.at[i])
        copy.start()
        copies.append(copy)
    for copy in copies:
        copy.wait()


def store_later_kernel(mine, other, out, rows, sems):
    @pl.when(core_index() == 1)
    def _():
        copies = []
        for i, (x, at) in enumerate(((mine, 0), (mine, W), (other, 0), (other, W))):
            rows[i] = x[:, at : at + W]
            copy = pltpu.make_async_copy(rows.at[i], out.at[(2, 3, 0, 1)[i]], sems.at[i])
            copy.start()
            copies.append(copy)
        for copy in copies:
            copy.wait()


def store_earlier_kernel(pair, x, part, out, rows, sems):
    del part

    @pl.when(core_index() == 0)
    def _():
        unpack_rows(x, out, rows, sems, pair)


def store(kernel, arrays, *part):
    return call(
        kernel,
        jax.ShapeDtypeStruct((4, C, W), BF16),
        len(arrays) + len(part),
        "store",
        scratch=[pltpu.VMEM((4, C, W), BF16), pltpu.SemaphoreType.DMA((4,))],
        moved=500000,
        in_specs=[VMEM] * len(arrays) + [ANY] * len(part),
        out_specs=ANY,
        aliases={len(arrays): 0} if part else None,
    )(*arrays, *part)


def tiles_of(x):
    return [x[:, t * LANES : (t + 1) * LANES] for t in range(x.shape[1] // LANES)]


def activate(x, gain, valid):
    x = x.astype(F32)
    scale = lax.rsqrt(jnp.sum(x * x, axis=0, keepdims=True) * (1.0 / C) + EPS)
    if valid is not None:
        scale = scale * valid
    h = x * scale * gain
    return (h + h * jnp.tanh(h)).astype(BF16)


def between(x, y):
    low = lax.broadcasted_iota(jnp.int32, (1, LANES), 1) < LANES // 2
    turned = [pltpu.roll(t, LANES // 2, 1) for t in x[2:] + y[:3]]
    return [jnp.where(low, turned[i], turned[i + 1]) for i in range(5)]


def stack(rows, at, x, y):
    for t, (above, middle, below) in enumerate(zip(x, between(x, y), y)):
        lanes = slice(at + t * LANES, at + (t + 1) * LANES)
        rows[:C, lanes] = above
        rows[C : 2 * C, lanes] = middle
        rows[2 * C :, lanes] = below


def put(rows, tiles, place, at=0):
    for t, x in enumerate(tiles):
        lanes = slice(at + t * LANES, at + (t + 1) * LANES)
        rows[place * C : (place + 1) * C, lanes] = x


def either(first, x, y):
    return [jnp.where(first, s, t) for s, t in zip(x, y)]


def middle(is0, far, near):
    return between(either(is0, far, near), either(is0, near, far))


def convolved(weight, rows):
    lane = lax.broadcasted_iota(jnp.int32, (1, LANES), 1)
    out = []
    for at in range(0, rows.shape[1], PAIR):
        product = jnp.dot(weight[...], rows[:, at : at + PAIR], preferred_element_type=F32)
        left, mid, right = (tiles_of(product[dj * C : (dj + 1) * C]) for dj in range(3))
        left = [pltpu.roll(t, 1, 1) for t in left]
        right = [pltpu.roll(t, LANES - 1, 1) for t in right]
        for t in range(5):
            a = jnp.where(lane == 0, left[t - 1] if t else 0.0, left[t])
            b = jnp.where(lane == LANES - 1, right[t + 1] if t < 4 else 0.0, right[t])
            if t == W // LANES:
                a = jnp.where(lane == W % LANES, 0.0, a)
                b = jnp.where(lane == W % LANES - 1, 0.0, b)
            out.append(mid[t] + a + b)
    return out


def inside(t):
    core, row = core_index(), lax.axis_index("rows")
    top = (core == 0) & (row == 0)
    bottom = (core == 1) & (row == lax.axis_size("rows") - 1)
    pixel = lax.broadcasted_iota(jnp.int32, (1, LANES), 1) + t * LANES
    outside = ((pixel < W) & top) | ((pixel >= W) & bottom)
    return jnp.where(outside, 0.0, 1.0).astype(F32)


def near_pick_kernel(pick, mine, owned, sib_o, w1, g1, w2, g2, part1, part2, s1, s2):
    is0 = core_index() == 0
    is_mine = core_index() == pick
    own = either(is_mine, tiles_of(mine.at[1]), tiles_of(owned.at[1]))
    sib = either(is_mine, tiles_of(mine.at[0]), tiles_of(sib_o))
    act = [activate(t, g1[...], None) for t in own]
    other = [activate(t, g1[...], None) for t in sib]
    none = [jnp.zeros_like(t) for t in act]
    put(s1, act, 0)
    put(s1, middle(is0, act, other), 1)
    put(s1, other, 2)
    inner = [activate(x.astype(BF16), g2[...], None) for x in convolved(w1, s1)]
    put(s2, middle(is0, none, act), 0)
    put(s2, act, 1)
    for t, x in enumerate(convolved(w1.at[:, C:], s2)):
        part1[:, t * LANES : (t + 1) * LANES] = x
    put(s2, middle(is0, none, inner), 0)
    put(s2, inner, 1)
    for t, (x, y) in enumerate(zip(own, convolved(w2.at[:, C:], s2))):
        part2[:, t * LANES : (t + 1) * LANES] = x.astype(F32) + y


def near(pick, mine, owned, sib_o, *weights):
    return call(
        functools.partial(near_pick_kernel, pick),
        [jax.ShapeDtypeStruct((C, PAIR), F32)] * 2,
        7,
        "near",
        scratch=[pltpu.VMEM((3 * C, PAIR), BF16), pltpu.VMEM((2 * C, PAIR), BF16)],
        flops=2 * C * C * 9 * PAIR,
        moved=2000000,
    )(mine, owned, sib_o, *weights)


def far_pick_kernel(pick, z, part1, part2, w1, g1, w2, g2, out, s2):
    is0 = core_index() == 0
    is_mine = core_index() == pick
    far = either(is_mine, tiles_of(z.at[1]), tiles_of(z.at[0]))
    far = [activate(t, g1[...], None) for t in far]
    none = [jnp.zeros_like(t) for t in far]
    put(s2, far, 0)
    put(s2, middle(is0, far, none), 1)
    inner = []
    for t, (x, y) in enumerate(zip(tiles_of(part1), convolved(w1.at[:, : 2 * C], s2))):
        inner.append(activate((x + y).astype(BF16), g2[...], inside(t)))
    put(s2, inner, 0)
    put(s2, middle(is0, inner, none), 1)
    for t, (x, y) in enumerate(zip(tiles_of(part2), convolved(w2.at[:, : 2 * C], s2))):
        out[:, t * LANES : (t + 1) * LANES] = (x + y).astype(BF16)


def far(pick, z, part1, part2, *weights):
    return call(
        functools.partial(far_pick_kernel, pick),
        pair_shape(),
        7,
        "far",
        scratch=[pltpu.VMEM((2 * C, PAIR), BF16)],
        flops=2 * C * C * 9 * 2 * PAIR,
        moved=4000000,
    )(z, part1, part2, *weights)


def spatial_body(z, own, sib, w1, g1, w2, g2, out, s1, s2):
    core, row = core_index(), lax.axis_index("rows")
    is0 = core == 0
    top = is0 & (row == 0)
    bottom = (core == 1) & (row == lax.axis_size("rows") - 1)
    gain = g1[...]
    above = [activate(t, gain, None) for t in either(is0, z, sib)]
    mid = [activate(t, gain, None) for t in own]
    below = [activate(t, gain, None) for t in either(is0, sib, z)]
    stack(s1, 0, above, mid)
    stack(s1, PAIR, mid, below)
    lane = lax.broadcasted_iota(jnp.int32, (1, LANES), 1)
    gain = g2[...]
    act = []
    for t, x in enumerate(convolved(w1, s1)):
        pixel = lane + t * LANES
        outside = ((pixel < W) & top) | ((pixel >= 3 * W) & bottom)
        act.append(activate(x.astype(BF16), gain, jnp.where(outside, 0.0, 1.0).astype(F32)))
    stack(s2, 0, act[:5], act[5:])
    for t, (x, y) in enumerate(zip(own, convolved(w2, s2))):
        out[:, t * LANES : (t + 1) * LANES] = (x.astype(F32) + y).astype(BF16)


def spatial_kernel(z, own, sib, *rest):
    spatial_body(tiles_of(z), tiles_of(own), tiles_of(sib), *rest)


def spatial_pick_kernel(pick, z, mine, owned, sib_o, *rest):
    is_mine = core_index() == pick

    def chosen(x, y):
        return either(is_mine, tiles_of(x), tiles_of(y))

    spatial_body(
        chosen(z.at[1], z.at[0]), chosen(mine.at[1], owned.at[1]), chosen(mine.at[0], sib_o), *rest
    )


def spatial(kernel, n_in, name):
    return call(
        kernel,
        pair_shape(),
        n_in,
        name,
        scratch=[pltpu.VMEM((3 * C, 2 * PAIR), BF16), pltpu.VMEM((3 * C, PAIR), BF16)],
        flops=2 * C * C * 9 * 3 * PAIR,
        moved=4000000,
    )


def mixed(wt, x0, x1, x2):
    total = x0[...].astype(F32)
    for tap, x in enumerate((x0, x1, x2)):
        total = total + jnp.dot(
            wt[:, tap * C : (tap + 1) * C], x[...], preferred_element_type=F32
        )
    return total.astype(BF16)


def temporal_kernel(wt, x0, x1, x2, out):
    out[...] = mixed(wt, x0, x1, x2)


def temporal(wt, x0, x1, x2):
    return call(
        temporal_kernel, pair_shape(), 4, "temporal", flops=2 * C * C * 3 * PAIR, moved=1300000
    )(wt, x0, x1, x2)


def temporal_late_kernel(wt, x0, x1, x2, y0, out, part):
    out[...] = mixed(wt, x0, x1, x2)
    total = y0[...].astype(F32)
    for tap, y in enumerate((y0, x2)):
        total = total + jnp.dot(
            wt[:, tap * C : (tap + 1) * C], y[...], preferred_element_type=F32
        )
    part[...] = total


def temporal_last_kernel(wt, part, y2, out):
    last = jnp.dot(wt[:, 2 * C :], y2[...], preferred_element_type=F32)
    out[...] = (part[...] + last).astype(BF16)


def on_device(video, spatial_weights, norm_gains, temporal_weights):
    frames, rows = lax.axis_size("frames"), lax.axis_size("rows")
    swaps = [(i, i ^ 1) for i in range(frames)]
    across = []
    for f in range(frames):
        for r in range(rows):
            to = r + 1 if f % 2 else r - 1
            if 0 <= to < rows:
                across.append((f * rows + r, (f ^ 1) * rows + to))
    later = [(i, i + 2) for i in range(frames - 2)]

    def swap(x):
        return lax.ppermute(x, "frames", swaps)

    def halo(x):
        return lax.ppermute(x, ("frames", "rows"), across)

    def onward(x):
        return lax.ppermute(x, "frames", later)

    raw = jnp.transpose(video[0], (0, 2, 1))
    view = in_hbm(raw)
    mine = call(
        pack_kernel,
        jax.ShapeDtypeStruct((2, C, PAIR), BF16),
        1,
        "pack",
        scratch=[pltpu.VMEM((4, C, W), BF16), pltpu.SemaphoreType.DMA((4,))],
        moved=1000000,
        in_specs=[ANY],
    )(view)
    arrived = pltpu.with_memory_space_constraint(swap(raw), pltpu.VMEM)
    owned, sib_o = call(join_kernel, [jax.ShapeDtypeStruct((2, C, PAIR), BF16), pair_shape()], 2, "join", moved=1000)(
        mine, arrived
    )
    z = halo(owned)
    (w0, w1, w2, w3, far0, far1), (g0, g1, g2, g3), ts = prepare(spatial_weights, norm_gains, temporal_weights)

    block = (w0, g0, w1, g1)
    by_core = (far0, g0, far1, g1)
    parts = near(1, mine, owned, sib_o, *by_core)
    inner_b = far(1, z, *parts, *by_core)
    before_b = onward(inner_b)
    inner_a = spatial(functools.partial(spatial_pick_kernel, 0), 8, "spatial_a1")(z, mine, owned, sib_o, *block)
    before_a = onward(inner_a)

    own_b = temporal(ts[0], inner_b, inner_a, before_b)
    z_b, sib_b = halo(own_b), swap(own_b)
    own_a = temporal(ts[0], inner_a, before_b, before_a)
    z_a, sib_a = halo(own_a), swap(own_a)
    both = (w2, g2, w3, g3)
    inner_b = spatial(spatial_kernel, 7, "spatial_b")(z_b, own_b, sib_b, *both)
    before_b = onward(inner_b)
    inner_a = spatial(spatial_kernel, 7, "spatial_a")(z_a, own_a, sib_a, *both)
    before_a = onward(inner_a)
    late, part = call(
        temporal_late_kernel,
        [pair_shape(), jax.ShapeDtypeStruct((C, PAIR), F32)],
        5,
        "temporal_late",
        moved=2000000,
    )(ts[1], inner_b, inner_a, before_b, inner_a)
    late_other = swap(late)
    out = store(store_later_kernel, (late, late_other))
    early = call(temporal_last_kernel, pair_shape(), 3, "temporal_last", moved=1500000)(ts[1], part, before_a)
    early_other = swap(early)
    out = store(functools.partial(store_earlier_kernel, 0), (early,), out)
    out = store(functools.partial(store_earlier_kernel, 1), (early_other,), out)
    return jnp.transpose(out, (0, 2, 1))[None]


def solution(mesh):
    placed = (P("frames", "rows", None, None), P(), P(), P())
    return jax.shard_map(
        on_device,
        mesh=mesh,
        in_specs=placed,
        out_specs=P("frames", "rows", None, None),
        check_vma=False,
    )
```
